32 devices in a mesh: dp: 8 (over z, y), mp: 4 (over x, core).
Axes of the slice: x: 2, y: 2, z: 4, core: 2. Of those that a mesh axis runs over, the one named last changes fastest.
Arguments:
- hot_ids: int32 [8192, 7], P('dp'), may hold values from 0 to 1023
- touched: int32 [8, 4, 256], P('dp', 'mp'), may hold values from 0 to 8191, as said below
- cold_items: int32 [8, 4, 2048], P('dp', 'mp'), may hold values from 0 to 255
- bag_counts: int32 [8, 4, 1024], P('dp', 'mp'), may hold values from 1 to 8, 2048 in all within a row
- owner_map: int32 [8192], replicated, may hold values from 0 to 8191, as said below
- grad_out: bfloat16 [8192, 256], P('dp'), may hold values from -6 to 6
- weight_in: bfloat16 [1024, 512], P(None, 'mp'), may hold values from -0.1875 to 0.1875
- bias_in: float32 [512], P('mp'), may hold values from -4 to 4
- weight_out: bfloat16 [512, 256], P('mp'), may hold values from -0.25 to 0.25
- hot_table: float32 [1024, 128], replicated, may hold values from -6 to 6
- hot_accum: float32 [1024, 128], replicated, may hold values from 0.25 to 4
- cold_table: float32 [8192, 128], P(('dp', 'mp')), may hold values from -6 to 6
- cold_accum: float32 [8192, 128], P(('dp', 'mp')), may hold values from 0.25 to 4
Outputs:
- hot_updated: float32 [1024, 128], replicated
- hot_accum_new: float32 [1024, 128], replicated
- cold_updated: float32 [8192, 128], P(('dp', 'mp'))
- cold_accum_new: float32 [8192, 128], P(('dp', 'mp'))
The draws below stay inside these ranges and needn't reach their ends.
Inputs may be any that keep to these rules, and one draw needn't show every extreme that they name: owner_map is a permutation of the cold row ids: cold row g is stored in row owner_map[g] of cold_table. `touched`: the 256 ids of one device are distinct, and owner_map sends all of them to rows stored on devices with the same mp index as that device; at most 64 of them are stored on any one dp index, and exactly 64 on some.
All inputs are finite; a program needn't handle non-finite values.
Results may differ from the reference program's by a relative error of at most 0.0038.
Values may be sent and summed in bfloat16 or wider, within the bound.
No kernel may reach another device: no remote copies, remote signals or barrier semaphores. Data moves between devices by JAX's collectives and lax.ppermute only.
A program may use at most 64 MiB of HBM per device.

```python
import math
import jax
import jax.numpy as jnp
import numpy as np
from jax import lax

E = 128
HOTF = 7
D_IN = 1024
H1 = 512
H2 = 256
B = 1024
HOT = 1024
SLOTS = 256
TOUCH = 256
MOSTBAG = 8
ITEMS = 2048
COLD = 8192
N_DP = 8
N_MP = 4


def storage_order(key):
    return jax.random.permutation(jax.random.fold_in(key, 11), COLD).astype(jnp.int32)


def draw_owner_map(key, part):
    return storage_order(key)


def draw_touched(key, part):
    placed = storage_order(key)
    inverse = jnp.zeros((COLD,), jnp.int32).at[placed].set(jnp.arange(COLD, dtype=jnp.int32))
    hot_count = max(1, N_DP // 16)
    capacity = 2 * TOUCH // N_DP
    rest_count = TOUCH - hot_count * capacity
    other_count = N_DP - hot_count
    base_count = rest_count // other_count
    extra_count = rest_count - base_count * other_count
    owner_iota = jnp.arange(N_DP, dtype=jnp.int32)
    scores = jax.random.randint(jax.random.fold_in(key, 21), (N_MP, N_DP), 0, 1 << 20, dtype=jnp.int32) * N_DP + owner_iota
    rank_of = jnp.argsort(jnp.argsort(scores, axis=1), axis=1).astype(jnp.int32)
    is_hot = (rank_of < hot_count).astype(jnp.int32)
    extra_scores = jax.random.randint(jax.random.fold_in(key, 22), (N_DP, N_MP, N_DP), 0, 1 << 20, dtype=jnp.int32) * N_DP + owner_iota + is_hot[None, :, :] * (1 << 30)
    extra_rank = jnp.argsort(jnp.argsort(extra_scores, axis=2), axis=2).astype(jnp.int32)
    gets_extra = (extra_rank < extra_count).astype(jnp.int32)
    counts = jnp.where(is_hot[None, :, :] == 1, capacity, base_count + gets_extra).astype(jnp.int32)
    end_pos = jnp.cumsum(counts, axis=2).astype(jnp.int32)
    offsets = (end_pos - counts).astype(jnp.int32)
    touch_iota = jnp.arange(TOUCH, dtype=jnp.int32)
    owner_of = jax.vmap(lambda ends: jnp.searchsorted(ends, touch_iota, side='right'))(end_pos.reshape(-1, N_DP)).astype(jnp.int32).reshape(N_DP, N_MP, TOUCH)
    within = touch_iota[None, None, :] - jnp.take_along_axis(offsets, owner_of, axis=2)
    start_slot = jax.random.randint(jax.random.fold_in(key, 23), (N_DP, N_MP, N_DP), 0, SLOTS, dtype=jnp.int32)
    slot_of = (jnp.take_along_axis(start_slot, owner_of, axis=2) + within) % SLOTS
    mp_iota = jnp.arange(N_MP, dtype=jnp.int32)
    position = (owner_of * N_MP + mp_iota[None, :, None]) * SLOTS + slot_of
    ids_sorted = inverse[position]
    shuffle_scores = jax.random.randint(jax.random.fold_in(key, 24), (N_DP, N_MP, TOUCH), 0, 1 << 20, dtype=jnp.int32) * TOUCH + touch_iota
    order_idx = jnp.argsort(shuffle_scores, axis=2).astype(jnp.int32)
    return jnp.take_along_axis(ids_sorted, order_idx, axis=2).astype(jnp.int32)


def touch_ends(result, stream_key, low, top_value):
    index_at = [jax.random.randint(jax.random.fold_in(stream_key, axis), (), 0, length) for axis, length in enumerate(result.shape)]
    longest = result.shape.index(max(result.shape))
    beside = index_at[:longest] + [(index_at[longest] + 1) % result.shape[longest]] + index_at[longest + 1:]
    return result.at[tuple(index_at)].set(low).at[tuple(beside)].set(top_value)


def level_of(rng, dims, cuts, low, largest):
    def one(dim, blocks):
        draws = jax.random.uniform(jax.random.fold_in(jax.random.fold_in(rng, 6), dim), (blocks,), jnp.float32, low / len(cuts), largest / len(cuts))
        return jnp.repeat(jnp.exp(draws), dims[dim] // blocks).reshape((-1,) + (1,) * (len(dims) - dim - 1))

    gain = one(*cuts[0])
    for cut in cuts[1:]:
        gain = gain * one(*cut)
    return gain


def rank_table(number_of, lean):
    portions = [(1 << 20) // math.isqrt(standing ** lean) + 1 for standing in range(1, number_of + 1)]
    deviation = 1 + sum(portions) // (1 << 30)
    return np.cumsum(np.array([max(1, weight // deviation) for weight in portions]))


def ranked(key, extent, count, slope):
    grid = rank_table(count, slope)
    lot = jax.random.randint(jax.random.fold_in(key, 1), extent, 0, int(grid[count - 1]))
    rank = jnp.searchsorted(jnp.asarray(grid, jnp.int32), lot, side="right")
    return jax.random.permutation(jax.random.fold_in(key, 2), count)[rank].astype(jnp.int32)


def length_profile(amount, total, bound, skew):
    portions = [(1 << 20) // math.isqrt(rank ** skew) + 1 for rank in range(2, amount + 1)]
    spare, given = total - bound - (amount - 1), [1] * (amount - 1)
    while spare > 0:
        movable = [i for i in range(amount - 1) if given[i] < bound]
        mass, left = sum([portions[i] for i in movable]), spare
        for i in movable:
            addition = min(bound - given[i], max(1, left * portions[i] // mass), spare)
            given[i] = given[i] + addition
            spare = spare - addition
    return np.array([bound] + given)


def uneven(key, number_of, total, bound, skew):
    if number_of == 2:
        one = jax.random.randint(key, (), max(1, total - bound), min(bound, total - 1) + 1)
        return jnp.stack([one, total - one])
    sizes = jnp.asarray(length_profile(number_of, total, bound, skew), jnp.int32)
    twos = (number_of - 1) // 2
    donor, taker = sizes[1:1 + 2 * twos:2], sizes[2:2 + 2 * twos:2]
    room = jnp.minimum(donor - 1, bound - taker)
    passed = jax.random.randint(jax.random.fold_in(key, 1), (twos,), 0, 1 << 20) % (room + 1)
    sizes = sizes.at[1:1 + 2 * twos:2].set(donor - passed).at[2:2 + 2 * twos:2].set(taker + passed)
    return sizes[jax.random.permutation(jax.random.fold_in(key, 2), number_of)]


def gaussian(rng, dims, width, bound, pieces=(), kind=jnp.bfloat16):
    result = width * jax.random.normal(rng, dims, jnp.float32)
    if pieces:
        result = result * level_of(rng, dims, pieces, -0.22, 0.18)
    return jnp.clip(result, -bound, bound).astype(kind)


def setup_inputs(seed: int = 0) -> dict:
    key_list = jax.random.split(jax.random.key(seed), 14)
    return {
        "hot_ids": touch_ends(ranked(key_list[0], (N_DP * B, HOTF), HOT, 2), jax.random.fold_in(key_list[0], 3), 0, HOT - 1).astype(jnp.int32),
        "touched": draw_touched(jax.random.fold_in(key_list[13], 71), 0),
        "cold_items": touch_ends(jax.random.randint(key_list[2], (N_DP, N_MP, ITEMS), 0, TOUCH), jax.random.fold_in(key_list[2], 1), 0, TOUCH - 1).astype(jnp.int32),
        "bag_counts": jax.vmap(lambda own: uneven(own, B, ITEMS, MOSTBAG, 2))(jax.random.split(key_list[3], N_DP * N_MP)).reshape((N_DP, N_MP, B)).astype(jnp.int32),
        "owner_map": draw_owner_map(jax.random.fold_in(key_list[13], 71), 0),
        "grad_out": gaussian(key_list[5], (N_DP * B, H2), 1.0, 6.0, ((0, 8),)),
        "weight_in": gaussian(key_list[6], (D_IN, H1), D_IN ** -0.5, 0.1875, ((1, 4),)),
        "bias_in": gaussian(key_list[7], (H1,), 1.0, 4.0, ((0, 4),), jnp.float32),
        "weight_out": gaussian(key_list[8], (H1, H2), H1 ** -0.5, 0.25, ((0, 4),)),
        "hot_table": gaussian(key_list[9], (HOT, E), 1.0, 6.0, (), jnp.float32),
        "hot_accum": jnp.clip(jnp.exp(jax.random.uniform(key_list[10], (HOT, E), jnp.float32, math.log(0.25), math.log(4.0))), 0.25, 4.0),
        "cold_table": gaussian(key_list[11], (COLD, E), 1.0, 6.0, ((0, 32),), jnp.float32),
        "cold_accum": jnp.clip(jnp.exp(math.log(4.0) - 2.7725887 * jax.random.uniform(key_list[12], (COLD, E), jnp.float32) ** level_of(key_list[12], (COLD, E), ((0, 32),), -0.2, 0.2)), 0.25, 4.0),
    }


STEP_SIZE = 0.5
HIGHEST = lax.Precision.HIGHEST

def adagrad(table_rows, accum_rows, grad_rows):
    accum_new = accum_rows + grad_rows * grad_rows
    return (table_rows - STEP_SIZE * grad_rows / jnp.sqrt(accum_new), accum_new)

def reference(hot_ids, touched, cold_items, bag_counts, owner_map, grad_out, weight_in, bias_in, weight_out, hot_table, hot_accum, cold_table, cold_accum):
    dp_count = touched.shape[0]
    hot_cols = HOTF * E
    ids_grouped = hot_ids.reshape(dp_count, B, HOTF)
    grads_grouped = grad_out.reshape(dp_count, B, H2)
    item_pos = jnp.arange(ITEMS, dtype=jnp.int32)
    touch_pos = jnp.arange(TOUCH, dtype=jnp.int32)

    def per_group(group_args):
        group_ids, group_grads, group_touched, group_items, group_counts = group_args
        stored_at = owner_map[group_touched]
        fetched = cold_table[stored_at]
        end_pos = jnp.cumsum(group_counts, axis=1).astype(jnp.int32)
        start_pos = (end_pos - group_counts).astype(jnp.int32)
        member = ((item_pos[None, None, :] >= start_pos[:, :, None]) & (item_pos[None, None, :] < end_pos[:, :, None])).astype(jnp.float32)
        picks = (group_items[:, :, None] == touch_pos[None, None, :]).astype(jnp.float32)
        count_mat = jnp.einsum('mbi,mit->mbt', member, picks, precision=HIGHEST)
        pooled = jnp.einsum('mbt,mte->be', count_mat, fetched, precision=HIGHEST)
        hot_rows = hot_table[group_ids].reshape(B, hot_cols)
        inputs = jnp.concatenate([hot_rows, pooled], axis=1).astype(jnp.bfloat16)
        pre_act = jnp.dot(inputs, weight_in, preferred_element_type=jnp.float32) + bias_in
        back_grad = jnp.dot(group_grads, weight_out.T, preferred_element_type=jnp.float32)
        sigmoid_val = jax.nn.sigmoid(pre_act)
        hidden_grad = (back_grad * sigmoid_val * (1.0 + pre_act * (1.0 - sigmoid_val))).astype(jnp.bfloat16)
        input_grad = jnp.dot(hidden_grad, weight_in.T, preferred_element_type=jnp.float32)
        hot_part = jax.ops.segment_sum(input_grad[:, :hot_cols].reshape(B * HOTF, E), group_ids.reshape(B * HOTF), num_segments=HOT)
        touch_grad = jnp.einsum('mbt,be->mte', count_mat, input_grad[:, hot_cols:], precision=HIGHEST)
        return (hot_part, stored_at.reshape(-1), touch_grad.reshape(-1, E))
    hot_parts, positions, touch_grads = lax.map(per_group, (ids_grouped, grads_grouped, touched, cold_items, bag_counts))
    hot_grad = lax.optimization_barrier(jnp.sum(hot_parts, axis=0))
    cold_grad = jax.ops.segment_sum(touch_grads.reshape(-1, E), positions.reshape(-1), num_segments=COLD)
    hot_updated, hot_accum_new = adagrad(hot_table, hot_accum, hot_grad)
    cold_updated, cold_accum_new = adagrad(cold_table, cold_accum, cold_grad)
    return (hot_updated, hot_accum_new, cold_updated, cold_accum_new)
```

```python
import jax
import jax.numpy as jnp
from jax import lax
from jax.experimental import pallas as pl
from jax.experimental.pallas import tpu as pltpu
from jax.sharding import PartitionSpec as P

STEP_SIZE = 0.5
F32 = jnp.float32
BF16 = jnp.bfloat16
I32 = jnp.int32


def adagrad(table_rows, accum_rows, grad_rows):
    accum_new = accum_rows + grad_rows * grad_rows
    return (table_rows - STEP_SIZE * grad_rows / jnp.sqrt(accum_new), accum_new)


def loop(count, body, init):
    if count <= 16:
        for i in range(count):
            init = body(i, init)
        return init
    return lax.fori_loop(0, count, body, init)


def hi_lo(x):
    hi = x.astype(BF16)
    lo = (x - hi.astype(F32)).astype(BF16)
    return jnp.concatenate([hi, lo], axis=1)


def sum_halves(x):
    half = x.shape[1] // 2
    return x[:, :half] + x[:, half:]


def dot(a, b, dims=(((1,), (0,)), ((), ()))):
    return lax.dot_general(a, b, dims, preferred_element_type=F32)


NT = (((1,), (1,)), ((), ()))


def iota(shape, dim, dtype=I32):
    r = lax.broadcasted_iota(I32, shape, dim)
    return r if dtype == I32 else r.astype(dtype)


VM = pl.BlockSpec(memory_space=pltpu.VMEM)
ANY = pl.BlockSpec(memory_space=pl.ANY)


def call(body, out_shapes, ins, name, specs=None, scratch=(), outs_specs=None):
    many = isinstance(out_shapes, (list, tuple))
    return pl.pallas_call(
        body,
        out_shape=out_shapes,
        in_specs=[VM] * len(ins) if specs is None else specs,
        out_specs=([VM] * len(out_shapes) if many else VM) if outs_specs is None else outs_specs,
        scratch_shapes=scratch,
        name=name,
    )(*ins)


def sds(shape, dtype):
    return jax.ShapeDtypeStruct(shape, dtype)


def hot_kernel(share, fields, ids_ref, idt_ref, table_ref, oht_ref, rows_ref):
    hot_rows, emb = table_ref.shape
    table = table_ref[...].astype(BF16)
    lane = iota((share, hot_rows), 1)
    sub = iota((hot_rows, share), 0)
    for f in range(fields):
        oh = (lane == ids_ref[:, f : f + 1]).astype(F32).astype(BF16)
        rows_ref[:, f * emb : (f + 1) * emb] = dot(oh, table).astype(BF16)
        oht_ref[:, f * share : (f + 1) * share] = (
            (sub == idt_ref[f : f + 1, :]).astype(F32).astype(BF16)
        )


def count_kernel(share, touch, item_rows, count_rows, pack_ref, cnt_ref, cntt_ref, pick_ref, memb_ref):
    mp_count = pack_ref.shape[0]
    lanes = pack_ref.shape[2]
    my = lax.axis_index("mp")
    per = share // lanes
    sub_t = iota((touch, lanes), 0, F32)
    sub_i = iota((lanes, share), 0, F32)

    def row(m, first):
        return jnp.concatenate(
            [pack_ref[m, pl.ds(first + my * per + j, 1), :] for j in range(per)], axis=1
        )

    for m in range(mp_count):
        starts = row(m, item_rows)
        ends = row(m, item_rows + count_rows)
        for c in range(item_rows):
            pick_ref[:, c * lanes : (c + 1) * lanes] = (
                (sub_t == pack_ref[m, c : c + 1, :]).astype(F32).astype(BF16)
            )
            at = sub_i + float(c * lanes)
            memb_ref[c * lanes : (c + 1) * lanes, :] = (
                ((at >= starts) & (at < ends)).astype(F32).astype(BF16)
            )
        counts_t = dot(pick_ref[...], memb_ref[...])
        cntt_ref[m * touch : (m + 1) * touch, :] = counts_t.astype(BF16)
        cnt_ref[:, m * touch : (m + 1) * touch] = counts_t.T.astype(BF16)


def bucket_kernel(dp_count, slots, cap, where_ref, pos_ref, q_ref, srow_ref):
    touch = where_ref.shape[1]
    lanes = pos_ref.shape[1]
    owner = where_ref[0:1, :]
    slot = where_ref[1:2, :]
    cols = jnp.broadcast_to(owner * slots + slot, (8, touch)).T
    pos_ref[...] = jnp.broadcast_to(cols[:, 0:1], (touch, lanes))
    owner_col = jnp.broadcast_to(owner, (8, touch)).T[:, 0:1]
    before = iota((touch, touch), 0) < iota((touch, touch), 1)
    rank = jnp.sum(
        ((owner_col == owner) & before).astype(F32), axis=0, keepdims=True
    )
    bucket = owner.astype(F32) * float(cap) + rank
    q_ref[...] = (iota((dp_count * cap, touch), 0, F32) == bucket).astype(F32).astype(BF16)
    rank_col = jnp.broadcast_to(rank, (8, touch)).T[:, 0:1]
    at_rank = (iota((touch, lanes), 1, F32) == rank_col).astype(F32)
    mine = jnp.where(iota((dp_count * 8, touch), 0) // 8 == owner, slot.astype(F32), 0.0)
    srow_ref[...] = lax.dot_general(
        mine,
        at_rank,
        (((1,), (0,)), ((), ())),
        precision=lax.Precision.HIGHEST,
        preferred_element_type=F32,
    )


def fetch_kernel(pos_ref, table_ref, out_ref):
    owners, slots, emb = table_ref.shape
    touch, lanes = pos_ref.shape
    lane = iota((touch, lanes), 1)

    def body(o, acc):
        rel = pos_ref[...] - o * slots
        hit = jnp.concatenate(
            [
                (lane + j * lanes == rel).astype(F32).astype(BF16)
                for j in range(slots // lanes)
            ],
            axis=1,
        )
        return acc + dot(hit, table_ref[o])

    out_ref[...] = loop(owners, body, jnp.zeros((touch, emb), F32)).astype(BF16)


def pre_kernel(
    share, d_in, w0, w1, w2, w3, pack_ref, grads_ref, rows_ref, wt_ref, tail_ref, pre_ref, back_ref
):
    my = lax.axis_index("mp")
    emb = w0.shape[1]
    hot_cols = rows_ref.shape[1]
    bias_row = pack_ref.shape[1] - 8
    grads = grads_ref[pl.ds(pl.multiple_of(my * share, share), share), :]
    rows = rows_ref[...]
    for k, w in enumerate((w0, w1, w2, w3)):
        at = slice(k * emb, (k + 1) * emb)
        bias = pack_ref[my ^ k, bias_row : bias_row + 1, :]
        pre_ref[:, at] = dot(rows, w[:hot_cols, :]) + bias
        acc = jnp.zeros((share, emb), F32)
        for j in range(grads.shape[1] // emb):
            piece = w[d_in + j * emb : d_in + (j + 1) * emb, :]
            acc = acc + dot(grads[:, j * emb : (j + 1) * emb], piece, NT)
        back_ref[:, at] = acc
        tail_ref[:, at] = w[hot_cols:d_in, :]
        wt_ref[at, :] = w[:d_in, :].astype(F32).T.astype(BF16)


def main_kernel(
    fields,
    cnt_ref,
    fetched_ref,
    pre_ref,
    back_ref,
    tail_ref,
    wt_ref,
    cntt_ref,
    oht_hbm,
    hot_send,
    hot_keep,
    touch_send,
    touch_keep,
    oht_ref,
    ig_ref,
    sem,
):
    copy = pltpu.make_async_copy(oht_hbm, oht_ref, sem)
    copy.start()
    emb = fetched_ref.shape[1]
    share = cnt_ref.shape[0]
    core = lax.axis_index("mp") % 2
    pooled = dot(cnt_ref[...], fetched_ref[...]).astype(BF16)
    pre = pre_ref[...] + dot(pooled, tail_ref[...])
    sig = jax.nn.sigmoid(pre)
    hidden = (back_ref[...] * sig * (1.0 + pre * (1.0 - sig))).astype(BF16)
    grad = dot(hidden, wt_ref[...])
    for f in range(fields):
        ig_ref[f * share : (f + 1) * share, :] = hi_lo(grad[:, f * emb : (f + 1) * emb])
    bag = hi_lo(grad[:, fields * emb :])
    copy.wait()
    half = hot_send.shape[0]
    for ref, c in ((hot_send, 1 - core), (hot_keep, core)):
        first = pl.multiple_of(c * half, half)
        ref[...] = sum_halves(dot(oht_ref[pl.ds(first, half), :], ig_ref[...]))
    groups, touch, _ = touch_send.shape
    for x in range(groups):
        for ref, c in ((touch_send, 1 - core), (touch_keep, core)):
            first = pl.multiple_of((2 * x + c) * touch, touch)
            ref[x] = sum_halves(dot(cntt_ref[pl.ds(first, touch), :], bag))


def reduce_kernel(parts_ref, out_ref):
    total = jnp.sum(parts_ref[...], axis=0, keepdims=True)
    out_ref[...] = jnp.broadcast_to(total, out_ref.shape)


def pack_kernel(cap, keep_ref, got_ref, q_ref, srow_ref, out_ref):
    owners = out_ref.shape[0]
    emb = out_ref.shape[2]
    both = hi_lo(keep_ref[...] + got_ref[...])
    rows = sum_halves(dot(q_ref[...], both))
    out_ref[:, :cap, :] = rows.reshape(owners, cap, emb)
    out_ref[:, cap:, :] = srow_ref[...].reshape(owners, 8, emb)


def cold_kernel(cap, arrived_ref, table_ref, accum_ref, new_ref, acc_ref):
    slots, emb = table_ref.shape
    sub = iota((slots, cap), 0, F32)

    def body(d, acc):
        slot = arrived_ref[d, cap : cap + 1, :][:, :cap]
        hit = (sub == slot).astype(F32).astype(BF16)
        return acc + dot(hit, hi_lo(arrived_ref[d, :cap, :]))

    grad = sum_halves(loop(arrived_ref.shape[0], body, jnp.zeros((slots, 2 * emb), F32)))
    new_ref[...], acc_ref[...] = adagrad(table_ref[...], accum_ref[...], grad)


def final_kernel(mine_ref, theirs_ref, table_ref, accum_ref, new_ref, acc_ref):
    half = mine_ref.shape[0]
    core = lax.axis_index("mp") % 2
    for ref, c in ((mine_ref, core), (theirs_ref, 1 - core)):
        at = pl.ds(pl.multiple_of(c * half, half), half)
        new_ref[at, :], acc_ref[at, :] = adagrad(table_ref[at, :], accum_ref[at, :], ref[...])


def per_device(
    hot_ids,
    touched,
    cold_items,
    bag_counts,
    owner_map,
    grad_out,
    weight_in,
    bias_in,
    weight_out,
    hot_table,
    hot_accum,
    cold_table,
    cold_accum,
):
    dp_count = lax.axis_size("dp")
    mp_count = lax.axis_size("mp")
    my_mp = lax.axis_index("mp")
    slots, emb = cold_table.shape
    samples, fields = hot_ids.shape
    touch = touched.shape[2]
    items = cold_items.shape[2]
    d_in = weight_in.shape[0]
    hidden = weight_in.shape[1]
    hot_rows = hot_table.shape[0]
    share = samples // mp_count
    cap = -(-(2 * touch // dp_count) // 8) * 8
    both = ("dp", "mp")

    def swap(x, mask):
        return lax.ppermute(x, "mp", [(i, i ^ mask) for i in range(mp_count)])

    with jax.named_scope("tables"):
        mine = jnp.broadcast_to(cold_table.astype(BF16)[None], (dp_count, slots, emb))
        tables = lax.all_to_all(mine, "dp", split_axis=0, concat_axis=0, tiled=True)

    with jax.named_scope("weights"):
        w0 = jnp.concatenate(
            [weight_in] + [weight_out[:, j : j + emb] for j in range(0, weight_out.shape[1], emb)],
            axis=0,
        )
        w2 = swap(w0, 2)
        w1 = swap(w0, 1)
        w3 = swap(w2, 1)

    with jax.named_scope("small"):
        ends = jnp.cumsum(bag_counts[0, 0])
        pack = jnp.concatenate(
            [
                cold_items[0, 0].astype(F32).reshape(items // emb, emb),
                (ends - bag_counts[0, 0]).astype(F32).reshape(samples // emb, emb),
                ends.astype(F32).reshape(samples // emb, emb),
                jnp.pad(bias_in.reshape(1, emb), ((0, 7), (0, 0))),
            ],
            axis=0,
        )
        packs = lax.all_gather(pack, "mp", axis=0)

    with jax.named_scope("buckets"):
        stored = owner_map[touched[0, 0]]
        where = jnp.stack([stored // (mp_count * slots), stored % slots])
        pos, q_mat, slot_rows = call(
            lambda *r: bucket_kernel(dp_count, slots, cap, *r),
            [
                sds((touch, emb), I32),
                sds((dp_count * cap, touch), BF16),
                sds((dp_count * 8, emb), F32),
            ],
            [where],
            "buckets",
        )

    with jax.named_scope("hot"):
        ids = lax.dynamic_slice_in_dim(hot_ids, my_mp * share, share, 0)
        oht, rows = call(
            lambda *r: hot_kernel(share, fields, *r),
            [sds((hot_rows, fields * share), BF16), sds((share, fields * emb), BF16)],
            [ids, ids.T, hot_table],
            "hot",
        )

    with jax.named_scope("counts"):
        cnt, cntt = call(
            lambda *r: count_kernel(share, touch, items // emb, samples // emb, *r),
            [sds((share, mp_count * touch), BF16), sds((mp_count * touch, share), BF16)],
            [packs],
            "counts",
            scratch=[pltpu.VMEM((touch, items), BF16), pltpu.VMEM((items, share), BF16)],
        )

    with jax.named_scope("pre"):
        wt, tail, pre, back = call(
            lambda *r: pre_kernel(share, d_in, *r),
            [
                sds((mp_count * hidden, d_in), BF16),
                sds((emb, mp_count * hidden), BF16),
                sds((share, mp_count * hidden), F32),
                sds((share, mp_count * hidden), F32),
            ],
            [w0, w1, w2, w3, packs, grad_out, rows],
            "pre",
        )

    with jax.named_scope("fetch"):
        fetched = call(fetch_kernel, sds((touch, emb), BF16), [pos, tables], "fetch")
        fetched_all = lax.all_gather(fetched, "mp", axis=0, tiled=True)

    with jax.named_scope("main"):
        groups = mp_count // 2
        hot_send, hot_keep, touch_send, touch_keep = call(
            lambda *r: main_kernel(fields, *r),
            [sds((hot_rows // 2, emb), F32)] * 2 + [sds((groups, touch, emb), F32)] * 2,
            [cnt, fetched_all, pre, back, tail, wt, cntt, oht],
            "main",
            specs=[VM] * 7 + [ANY],
            scratch=[
                pltpu.VMEM((hot_rows, fields * share), BF16),
                pltpu.VMEM((fields * share, 2 * emb), BF16),
                pltpu.SemaphoreType.DMA,
            ],
        )

    with jax.named_scope("hotsum"):
        group_size = dp_count * groups
        rank_groups = [[g * 2 + c for g in range(group_size)] for c in range(2)]

        def exchange(x):
            return lax.all_to_all(
                x, both, split_axis=0, concat_axis=0, tiled=True, axis_index_groups=rank_groups
            )

        chip = hot_keep + swap(hot_send, 1)
        parts = exchange(chip.reshape(group_size, -1, emb))
        shard = call(reduce_kernel, sds(parts.shape, F32), [parts], "hotsum")
        half = exchange(shard).reshape(hot_rows // 2, emb)
        other = swap(half, 1)
        hot_updated, hot_accum_new = call(
            final_kernel,
            [sds(hot_table.shape, F32)] * 2,
            [half, other, hot_table, hot_accum],
            "hotout",
        )

    with jax.named_scope("cold"):
        mine = touch_keep + swap(touch_send, 1)
        my_x = my_mp // 2
        keep = lax.dynamic_index_in_dim(mine, my_x, 0, keepdims=False)
        give = lax.dynamic_index_in_dim(mine, 1 - my_x, 0, keepdims=False)
        got = swap(give, 2)
        outgoing = call(
            lambda *r: pack_kernel(cap, *r),
            sds((dp_count, cap + 8, emb), F32),
            [keep, got, q_mat, slot_rows],
            "coldpack",
        )
        arrived = lax.all_to_all(outgoing, "dp", split_axis=0, concat_axis=0, tiled=True)
        cold_updated, cold_accum_new = call(
            lambda *r: cold_kernel(cap, *r),
            [sds(cold_table.shape, F32)] * 2,
            [arrived, cold_table, cold_accum],
            "coldout",
        )
    return (hot_updated, hot_accum_new, cold_updated, cold_accum_new)


def solution(mesh):
    return jax.shard_map(
        per_device,
        mesh=mesh,
        in_specs=(
            P("dp", None),
            P("dp", "mp", None),
            P("dp", "mp", None),
            P("dp", "mp", None),
            P(),
            P("dp", None),
            P(None, "mp"),
            P("mp"),
            P("mp", None),
            P(),
            P(),
            P(("dp", "mp"), None),
            P(("dp", "mp"), None),
        ),
        out_specs=(P(), P(), P(("dp", "mp"), None), P(("dp", "mp"), None)),
        check_vma=False,
    )
```

```python
import jax
import jax.numpy as jnp
from jax import lax
from jax.experimental import pallas as pl
from jax.experimental.pallas import tpu as pltpu
from jax.sharding import PartitionSpec as P

STEP_SIZE = 0.5
F32 = jnp.float32
BF16 = jnp.bfloat16
I32 = jnp.int32


def adagrad(table_rows, accum_rows, grad_rows):
    accum_new = accum_rows + grad_rows * grad_rows
    return (table_rows - STEP_SIZE * grad_rows / jnp.sqrt(accum_new), accum_new)


def loop(count, body, init):
    if count <= 16:
        for i in range(count):
            init = body(i, init)
        return init
    return lax.fori_loop(0, count, body, init)


def hi_lo(x):
    hi = x.astype(BF16)
    lo = (x - hi.astype(F32)).astype(BF16)
    return jnp.concatenate([hi, lo], axis=1)


def sum_halves(x):
    half = x.shape[1] // 2
    return x[:, :half] + x[:, half:]


def dot(a, b, dims=(((1,), (0,)), ((), ()))):
    return lax.dot_general(a, b, dims, preferred_element_type=F32)


NT = (((1,), (1,)), ((), ()))


def iota(shape, dim, dtype=I32):
    r = lax.broadcasted_iota(I32, shape, dim)
    return r if dtype == I32 else r.astype(dtype)


VM = pl.BlockSpec(memory_space=pltpu.VMEM)


def call(body, outs, ins, scratch=(), late=()):
    avals = [
        pltpu.VMEM(shape, dtype) if stay else jax.ShapeDtypeStruct(shape, dtype)
        for shape, dtype, stay in outs
    ]
    return pl.pallas_call(
        body,
        out_shape=avals,
        in_specs=[VM] * len(ins),
        out_specs=[VM] * len(outs),
        scratch_shapes=scratch,
        compiler_params=pltpu.CompilerParams(vmem_limit_bytes=16 * 1024 * 1024),
    )(
        *[
            pltpu.with_memory_space_constraint(x, pltpu.HBM if i in late else pltpu.VMEM)
            for i, x in enumerate(ins)
        ]
    )


def column(row):
    return jnp.broadcast_to(row, (8, row.shape[1])).T[:, 0:1]


def cast_kernel(table_ref, out_ref):
    out_ref[...] = table_ref[...].astype(BF16)


def spread_kernel(table_ref, out_ref):
    table = table_ref[...].astype(BF16)
    for o in range(out_ref.shape[0]):
        out_ref[o] = table


def pack_rows(d_in, out_width, hidden, emb, item_rows):
    starts = [0, d_in, d_in + out_width // emb * hidden]
    starts.append(starts[-1] + -(-item_rows // 16) * 16)
    starts.append(starts[-1] + 16)
    return starts + [starts[-1] + 16]


def prep_kernel(at, w_ref, v_ref, items_ref, sizes_ref, bias_ref, out_ref):
    hidden, width = v_ref.shape
    emb = out_ref.shape[1]
    out_ref[at[0] : at[1], :] = w_ref[...]
    for j in range(width // emb):
        out_ref[at[1] + j * hidden : at[1] + (j + 1) * hidden, :] = v_ref[
            :, j * emb : (j + 1) * emb
        ]

    def padded(x, rows):
        if x.shape[0] == rows:
            return x
        return jnp.concatenate([x, jnp.zeros((rows - x.shape[0], emb), F32)], axis=0)

    items = items_ref[...].astype(F32)
    out_ref[at[2] : at[3], :] = padded(items, at[3] - at[2]).astype(BF16)
    out_ref[at[3] : at[4], :] = padded(sizes_ref[...].astype(F32), 16).astype(BF16)
    bias = bias_ref[...]
    hi = bias.astype(BF16).astype(F32)
    mid = (bias - hi).astype(BF16).astype(F32)
    low = bias - hi - mid
    out_ref[at[4] : at[5], :] = padded(jnp.concatenate([hi, mid, low], axis=0), 16).astype(BF16)


def local_kernel(
    mp_count, slots, share, fields, map_ref, ids_ref, hot_ids_ref, hot_ref, pos_ref, rows_ref
):
    touch = ids_ref.shape[1]
    map_rows, lanes = map_ref.shape
    ids_col = column(ids_ref[...])
    in_row = (iota((touch, map_rows), 1) == ids_col // lanes).astype(F32)
    picked = lax.dot_general(
        in_row, map_ref[...].astype(F32), (((1,), (0,)), ((), ())),
        precision=lax.Precision.HIGHEST, preferred_element_type=F32,
    )
    in_lane = iota((touch, lanes), 1) == ids_col % lanes
    stored = jnp.sum(jnp.where(in_lane, picked, 0.0), axis=1, keepdims=True).astype(I32)
    stored = jnp.broadcast_to(stored, (touch, lanes))
    pos_ref[...] = stored // (mp_count * slots) * slots + stored % slots
    hot_rows, emb = hot_ref.shape
    hot = hot_ref[...].astype(BF16)
    my = lax.axis_index("mp")
    lane = iota((share, hot_rows), 1)
    for f in range(fields):
        mine = hot_ids_ref[f : f + 1, pl.ds(pl.multiple_of(my * share, share), share)]
        hit = (lane == column(mine)).astype(F32).astype(BF16)
        rows_ref[:, f * emb : (f + 1) * emb] = dot(hit, hot).astype(BF16)


def count_kernel(
    share, touch, at, item_rows, count_rows, p0, p1, p2, p3, cnt_ref, cntt_ref,
    items_ref, starts_ref, ends_ref, acc_ref,
):
    lanes = p0.shape[1]
    my = lax.axis_index("mp")
    per = share // lanes
    step = 2
    chunk = step * lanes
    sub_t = iota((touch, lanes), 0, F32)
    sub_i = iota((chunk, share), 0, F32)
    upto = (iota((lanes, lanes), 0) <= iota((lanes, lanes), 1)).astype(F32).astype(BF16)
    bounds = []
    for k, pack in enumerate((p0, p1, p2, p3)):
        sizes = pack[at[3] : at[4], :]
        ends = dot(sizes, upto)[:count_rows]
        sizes = sizes.astype(F32)[:count_rows]
        totals = jnp.broadcast_to(jnp.sum(sizes, axis=1, keepdims=True), ends.shape)
        row = iota(ends.shape, 0)
        for r in range(count_rows - 1):
            ends = ends + jnp.where(row > r, totals[r : r + 1, :], 0.0)
        ends_ref[k] = ends
        starts_ref[k] = ends - sizes
        items_ref[k] = pack[at[2] : at[3], :].astype(F32)[:item_rows]

    def rows_of(ref, k):
        return jnp.concatenate([ref[k, pl.ds(my * per + j, 1), :] for j in range(per)], axis=1)

    for k in range(4):
        starts = rows_of(starts_ref, k)
        ends = rows_of(ends_ref, k)
        low = jnp.min(starts).astype(I32)
        high = jnp.max(ends).astype(I32)
        bounds.append((starts, ends, low // chunk, (high + chunk - 1) // chunk))
    for k, (starts, ends, first, last) in enumerate(bounds):
        acc_ref[...] = jnp.zeros_like(acc_ref)

        def body(c, carry):
            pick = jnp.concatenate(
                [
                    (sub_t == items_ref[k, pl.ds(c * step + j, 1), :]).astype(F32).astype(BF16)
                    for j in range(step)
                ],
                axis=1,
            )
            pos = sub_i + (c * chunk).astype(F32)
            memb = ((pos >= starts) & (pos < ends)).astype(F32).astype(BF16)
            acc_ref[...] += dot(pick, memb)
            return carry

        lax.fori_loop(first, last, body, 0)
        counts_t = acc_ref[...]
        cntt_ref[k * touch : (k + 1) * touch, :] = counts_t.astype(BF16)
        cnt_ref[:, k * touch : (k + 1) * touch] = counts_t.T.astype(BF16)


def pre_kernel(
    share, at, hidden, p0, p1, p2, p3, grads_ref, rows_ref, wt_ref, tail_ref, pre_ref, back_ref
):
    my = lax.axis_index("mp")
    emb = p0.shape[1]
    hot_cols = rows_ref.shape[1]
    grads = grads_ref[pl.ds(pl.multiple_of(my * share, share), share), :]
    rows = rows_ref[...]
    for k, p in enumerate((p0, p1, p2, p3)):
        cols = slice(k * hidden, (k + 1) * hidden)
        bias = jnp.sum(p[at[4] : at[5], :].astype(F32), axis=0, keepdims=True)
        pre_ref[:, cols] = dot(rows, p[:hot_cols, :]) + bias
        back = jnp.zeros((share, hidden), F32)
        for j in range(grads.shape[1] // emb):
            piece = p[at[1] + j * hidden : at[1] + (j + 1) * hidden, :]
            back = back + dot(grads[:, j * emb : (j + 1) * emb], piece, NT)
        back_ref[:, cols] = back
        tail_ref[:, cols] = p[hot_cols : at[1], :]
        wt_ref[cols, :] = p[: at[1], :].astype(F32).T.astype(BF16)


def fetch_kernel(pos_ref, table_ref, out_ref):
    owners, slots, _ = table_ref.shape

    def body(o, acc):
        return acc + dot(hits(pos_ref, o * slots, slots), table_ref[o])

    out_ref[...] = loop(owners, body, jnp.zeros(out_ref.shape, F32)).astype(BF16)


def fetch_near_kernel(pos_ref, *refs):
    out_ref = refs[-1]
    slots = refs[0].shape[0]
    my = lax.axis_index("dp")
    acc = jnp.zeros(out_ref.shape, F32)
    for k, table in enumerate(refs[:-1]):
        acc = acc + dot(hits(pos_ref, (my ^ k) * slots, slots), table[...])
    out_ref[...] = acc.astype(BF16)


def hits(pos_ref, first, slots):
    rel = pos_ref[...] - first
    lane = iota(rel.shape, 1)
    lanes = rel.shape[1]
    return jnp.concatenate(
        [(lane + j * lanes == rel).astype(F32).astype(BF16) for j in range(slots // lanes)], axis=1
    )


def onehot_kernel(share, fields, slots, cap, ids_ref, pos_ref, out_ref, q_ref, srow_ref):
    my = lax.axis_index("mp")
    sub = iota((out_ref.shape[0], share), 0)
    for f in range(fields):
        mine = ids_ref[f : f + 1, pl.ds(pl.multiple_of(my * share, share), share)]
        out_ref[:, f * share : (f + 1) * share] = (sub == mine).astype(F32).astype(BF16)
    pos = pos_ref[...]
    touch, lanes = pos.shape
    row = pos.T[0:1, :]
    owner = row // slots
    before = iota((touch, touch), 0) < iota((touch, touch), 1)
    rank = jnp.sum(
        ((pos[:, 0:1] // slots == owner) & before).astype(F32), axis=0, keepdims=True
    )
    bucket = owner.astype(F32) * float(cap) + rank
    q_ref[...] = (iota(q_ref.shape, 0, F32) == bucket).astype(F32).astype(BF16)
    at_rank = (iota((touch, lanes), 1, F32) == column(rank)).astype(F32)
    mine = jnp.where(
        iota((srow_ref.shape[0], touch), 0) // 8 == owner, (row % slots).astype(F32), 0.0
    )
    srow_ref[...] = lax.dot_general(
        mine, at_rank, (((1,), (0,)), ((), ())),
        precision=lax.Precision.HIGHEST, preferred_element_type=F32,
    )


def main_kernel(
    fields, cnt_ref, f0, f1, f2, f3, pre_ref, back_ref, tail_ref, wt_ref, oht_ref,
    ig_ref, bag_ref, send_ref,
):
    touch, emb = f0.shape
    share = cnt_ref.shape[0]
    core = lax.axis_index("mp") % 2
    pooled = jnp.zeros((share, emb), F32)
    for k, f in enumerate((f0, f1, f2, f3)):
        pooled = pooled + dot(cnt_ref[:, k * touch : (k + 1) * touch], f[...])
    pre = pre_ref[...] + dot(pooled.astype(BF16), tail_ref[...])
    sig = jax.nn.sigmoid(pre)
    hidden = (back_ref[...] * sig * (1.0 + pre * (1.0 - sig))).astype(BF16)
    grad = dot(hidden, wt_ref[...])
    for f in range(fields):
        ig_ref[f * share : (f + 1) * share, :] = hi_lo(grad[:, f * emb : (f + 1) * emb])
    bag_ref[...] = hi_lo(grad[:, fields * emb :])
    half = send_ref.shape[0]
    first = pl.multiple_of((1 - core) * half, half)
    send_ref[...] = sum_halves(dot(oht_ref[pl.ds(first, half), :], ig_ref[...]))


def keep_kernel(oht_ref, ig_ref, bag_ref, cntt_ref, keep_ref, touch_send, touch_keep):
    half = keep_ref.shape[0]
    core = lax.axis_index("mp") % 2
    first = pl.multiple_of(core * half, half)
    keep_ref[...] = sum_halves(dot(oht_ref[pl.ds(first, half), :], ig_ref[...]))
    touch = touch_send.shape[1]
    for k in range(4):
        ref = touch_send if k % 2 else touch_keep
        rows = slice(k * touch, (k + 1) * touch)
        ref[k // 2] = sum_halves(dot(cntt_ref[rows, :], bag_ref[...]))


def add_kernel(a_ref, b_ref, out_ref):
    out_ref[...] = a_ref[...] + b_ref[...]


def pair_kernel(keep_ref, got_ref, mine_ref, give_ref):
    mine_ref[...] = keep_ref[0] + got_ref[0]
    give_ref[...] = keep_ref[1] + got_ref[1]


def fetch_kernel(pos_ref, table_ref, out_ref):
    owners, slots, emb = table_ref.shape
    touch, lanes = pos_ref.shape
    lane = iota((touch, lanes), 1)

    def body(o, acc):
        rel = pos_ref[...] - o * slots
        hit = jnp.concatenate(
            [
                (lane + j * lanes == rel).astype(F32).astype(BF16)
                for j in range(slots // lanes)
            ],
            axis=1,
        )
        return acc + dot(hit, table_ref[o])

    out_ref[...] = loop(owners, body, jnp.zeros((touch, emb), F32)).astype(BF16)


def reduce_kernel(parts_ref, out_ref):
    total = jnp.sum(parts_ref[...], axis=0, keepdims=True)
    out_ref[...] = jnp.broadcast_to(total, out_ref.shape)


def order_far_kernel(*refs):
    out_ref = refs[-1]
    far = lax.axis_index("dp") // 2
    for k, ref in enumerate(refs[:-1]):
        out_ref[far ^ k] = ref[0]


def order_near_kernel(*refs):
    out_ref = refs[-1]
    near = lax.axis_index("dp") % 2
    group = lax.axis_index("mp") // 2
    for k, ref in enumerate(refs[:-1]):
        for far in range(ref.shape[0]):
            out_ref[(far * 2 + (near ^ (k // 2))) * 2 + (group ^ (k % 2))] = ref[far]


def pack_kernel(cap, mine_ref, got_ref, q_ref, srow_ref, out_ref):
    owners = out_ref.shape[0]
    emb = out_ref.shape[2]
    rows = sum_halves(dot(q_ref[...], hi_lo(mine_ref[...] + got_ref[...])))
    out_ref[:, :cap, :] = rows.reshape(owners, cap, emb)
    out_ref[:, cap:, :] = srow_ref[...].reshape(owners, 8, emb)


def cold_kernel(cap, arrived_ref, table_ref, accum_ref, new_ref, acc_ref):
    slots, emb = table_ref.shape
    sub = iota((slots, cap), 0, F32)

    def body(d, acc):
        slot = arrived_ref[d, cap : cap + 1, :][:, :cap]
        hit = (sub == slot).astype(F32).astype(BF16)
        return acc + dot(hit, hi_lo(arrived_ref[d, :cap, :]))

    grad = sum_halves(loop(arrived_ref.shape[0], body, jnp.zeros((slots, 2 * emb), F32)))
    new_ref[...], acc_ref[...] = adagrad(table_ref[...], accum_ref[...], grad)


def final_kernel(mine_ref, theirs_ref, table_ref, accum_ref, new_ref, acc_ref):
    half = mine_ref.shape[0]
    core = lax.axis_index("mp") % 2
    for ref, c in ((mine_ref, core), (theirs_ref, 1 - core)):
        at = pl.ds(pl.multiple_of(c * half, half), half)
        new_ref[at, :], acc_ref[at, :] = adagrad(table_ref[at, :], accum_ref[at, :], ref[...])


def per_device(
    hot_ids,
    touched,
    cold_items,
    bag_counts,
    owner_map,
    grad_out,
    weight_in,
    bias_in,
    weight_out,
    hot_table,
    hot_accum,
    cold_table,
    cold_accum,
):
    dp_count = lax.axis_size("dp")
    mp_count = lax.axis_size("mp")
    slots, emb = cold_table.shape
    samples, fields = hot_ids.shape
    touch = touched.shape[2]
    items = cold_items.shape[2]
    d_in, hidden = weight_in.shape
    all_hidden = mp_count * hidden
    hot_rows = hot_table.shape[0]
    share = samples // mp_count
    cap = -(-(2 * touch // dp_count) // 8) * 8
    item_rows = items // emb
    count_rows = samples // emb
    both = ("dp", "mp")

    def swap(x, mask):
        return lax.ppermute(x, "mp", [(i, i ^ mask) for i in range(mp_count)])

    def far_swap(x, mask):
        return lax.ppermute(x, "dp", [(i, i ^ mask) for i in range(dp_count)])

    near = dp_count == 8 and mp_count == 4

    if near:
        (own,) = call(cast_kernel, [((slots, emb), BF16, True)], [cold_table], late=(0,))
        tables = [own] + [None] * 7
        for k in (4, 6, 2):
            tables[k] = far_swap(own, k)
        for k in (0, 4, 6, 2):
            tables[k + 1] = far_swap(tables[k], 1)
    else:
        (mine,) = call(
            spread_kernel, [((dp_count, slots, emb), BF16, False)], [cold_table], late=(0,)
        )
        tables = [lax.all_to_all(mine, "dp", split_axis=0, concat_axis=0, tiled=True)]

    at = pack_rows(d_in, weight_out.shape[1], hidden, emb, item_rows)
    (pack,) = call(
        lambda *r: prep_kernel(at, *r),
        [((at[-1], emb), BF16, True)],
        [
            weight_in,
            weight_out,
            cold_items.reshape(item_rows, emb),
            bag_counts.reshape(count_rows, emb),
            bias_in.reshape(1, hidden),
        ],
        late=range(5),
    )
    pack_far = swap(pack, 2)
    pack_near = swap(pack, 1)
    pack_cross = swap(pack_far, 1)
    packs = [pack, pack_near, pack_far, pack_cross]

    pos, rows = call(
        lambda *r: local_kernel(mp_count, slots, share, fields, *r),
        [((touch, emb), I32, True), ((share, fields * emb), BF16, True)],
        [owner_map.reshape(-1, emb), touched.reshape(1, touch), hot_ids.T, hot_table],
        late=range(4),
    )

    cnt, cntt = call(
        lambda *r: count_kernel(share, touch, at, item_rows, count_rows, *r),
        [
            ((share, mp_count * touch), BF16, True),
            ((mp_count * touch, share), BF16, True),
        ],
        packs,
        scratch=[
            pltpu.VMEM((mp_count, item_rows, emb), F32),
            pltpu.VMEM((mp_count, count_rows, emb), F32),
            pltpu.VMEM((mp_count, count_rows, emb), F32),
            pltpu.VMEM((touch, share), F32),
        ],
    )

    wt, tail, pre, back = call(
        lambda *r: pre_kernel(share, at, hidden, *r),
        [
            ((all_hidden, d_in), BF16, True),
            ((emb, all_hidden), BF16, True),
            ((share, all_hidden), F32, True),
            ((share, all_hidden), F32, True),
        ],
        [*packs, grad_out, rows],
        late=(4,),
    )

    (fetched,) = call(
        fetch_near_kernel if near else fetch_kernel,
        [((touch, emb), BF16, True)],
        [pos, *tables],
        late=() if near else (1,),
    )
    far = swap(fetched, 2)
    around = [fetched, swap(fetched, 1), far, swap(fetched, 3)]

    ids_late, _ = lax.optimization_barrier((hot_ids.T, fetched))
    oht, q_mat, slot_rows = call(
        lambda *r: onehot_kernel(share, fields, slots, cap, *r),
        [
            ((hot_rows, fields * share), BF16, True),
            ((dp_count * cap, touch), BF16, True),
            ((dp_count * 8, emb), F32, True),
        ],
        [ids_late, pos],
    )

    half_rows = hot_rows // 2
    ig, bag, hot_send = call(
        lambda *r: main_kernel(fields, *r),
        [
            ((fields * share, 2 * emb), BF16, True),
            ((share, 2 * emb), BF16, True),
            ((half_rows, emb), F32, True),
        ],
        [cnt, *around, pre, back, tail, wt, oht],
    )
    hot_got = swap(hot_send, 1)
    hot_keep, touch_send, touch_keep = call(
        keep_kernel,
        [
            ((half_rows, emb), F32, True),
            ((mp_count // 2, touch, emb), F32, True),
            ((mp_count // 2, touch, emb), F32, True),
        ],
        [oht, ig, bag, cntt],
    )

    group_size = dp_count * mp_count // 2
    rank_groups = [[g * 2 + c for g in range(group_size)] for c in range(2)]

    def exchange(x):
        return lax.all_to_all(
            x, both, split_axis=0, concat_axis=0, tiled=True, axis_index_groups=rank_groups
        )

    (chip,) = call(add_kernel, [((half_rows, emb), F32, True)], [hot_keep, hot_got])
    parts = exchange(chip.reshape(group_size, -1, emb))
    shard_shape = parts.shape if not near else (1, *parts.shape[1:])
    (shard,) = call(reduce_kernel, [(shard_shape, F32, True)], [parts])
    if near:
        pieces = [shard] + [far_swap(shard, 2 * k) for k in (1, 2, 3)]
        (line,) = call(order_far_kernel, [((4, *parts.shape[1:]), F32, True)], pieces)
        pieces = [line, swap(line, 2), far_swap(line, 1)]
        pieces.append(
            lax.ppermute(line, both, [(i, i ^ (mp_count + 2)) for i in range(dp_count * mp_count)])
        )
        (half,) = call(order_near_kernel, [(parts.shape, F32, True)], pieces)
        half = half.reshape(half_rows, emb)
    else:
        half = exchange(shard).reshape(half_rows, emb)
    other = swap(half, 1)
    hot_updated, hot_accum_new = call(
        final_kernel, [(hot_table.shape, F32, False)] * 2, [half, other, hot_table, hot_accum]
    )

    touch_got = swap(touch_send, 1)
    mine, give = call(pair_kernel, [((touch, emb), F32, True)] * 2, [touch_keep, touch_got])
    got = swap(give, 2)
    (outgoing,) = call(
        lambda *r: pack_kernel(cap, *r),
        [((dp_count, cap + 8, emb), F32, True)],
        [mine, got, q_mat, slot_rows],
    )
    arrived = lax.all_to_all(outgoing, "dp", split_axis=0, concat_axis=0, tiled=True)
    cold_updated, cold_accum_new = call(
        lambda *r: cold_kernel(cap, *r),
        [(cold_table.shape, F32, False)] * 2,
        [arrived, cold_table, cold_accum],
    )
    return (hot_updated, hot_accum_new, cold_updated, cold_accum_new)


def solution(mesh):
    return whole(mesh)


def whole(mesh):
    return jax.shard_map(
        per_device,
        mesh=mesh,
        in_specs=(
            P("dp", None),
            P("dp", "mp", None),
            P("dp", "mp", None),
            P("dp", "mp", None),
            P(),
            P("dp", None),
            P(None, "mp"),
            P("mp"),
            P("mp", None),
            P(),
            P(),
            P(("dp", "mp"), None),
            P(("dp", "mp"), None),
        ),
        out_specs=(P(), P(), P(("dp", "mp"), None), P(("dp", "mp"), None)),
        check_vma=False,
    )
```

```python
import jax
import jax.numpy as jnp
from jax import lax
from jax.experimental import pallas as pl
from jax.experimental.pallas import tpu as pltpu
from jax.sharding import PartitionSpec as P

STEP_SIZE = 0.5
F32 = jnp.float32
BF16 = jnp.bfloat16
I32 = jnp.int32


def adagrad(table_rows, accum_rows, grad_rows):
    accum_new = accum_rows + grad_rows * grad_rows
    return (table_rows - STEP_SIZE * grad_rows / jnp.sqrt(accum_new), accum_new)


def loop(count, body, init):
    if count <= 16:
        for i in range(count):
            init = body(i, init)
        return init
    return lax.fori_loop(0, count, body, init)


def hi_lo(x):
    hi = x.astype(BF16)
    lo = (x - hi.astype(F32)).astype(BF16)
    return jnp.concatenate([hi, lo], axis=1)


def sum_halves(x):
    half = x.shape[1] // 2
    return x[:, :half] + x[:, half:]


def dot(a, b, dims=(((1,), (0,)), ((), ()))):
    return lax.dot_general(a, b, dims, preferred_element_type=F32)


NT = (((1,), (1,)), ((), ()))
TN = (((0,), (0,)), ((), ()))


def iota(shape, dim, dtype=I32):
    r = lax.broadcasted_iota(I32, shape, dim)
    return r if dtype == I32 else r.astype(dtype)


VM = pl.BlockSpec(memory_space=pltpu.VMEM)


def call(body, outs, ins, scratch=(), late=()):
    avals = [
        pltpu.VMEM(shape, dtype) if stay else jax.ShapeDtypeStruct(shape, dtype)
        for shape, dtype, stay in outs
    ]
    return pl.pallas_call(
        body,
        out_shape=avals,
        in_specs=[VM] * len(ins),
        out_specs=[VM] * len(outs),
        scratch_shapes=scratch,
        compiler_params=pltpu.CompilerParams(vmem_limit_bytes=16 * 1024 * 1024),
    )(
        *[
            pltpu.with_memory_space_constraint(x, pltpu.HBM if i in late else pltpu.VMEM)
            for i, x in enumerate(ins)
        ]
    )


def column(row):
    return jnp.broadcast_to(row, (8, row.shape[1])).T[:, 0:1]


def cast_kernel(table_ref, out_ref):
    out_ref[...] = table_ref[...].astype(BF16)


def spread_kernel(table_ref, out_ref):
    table = table_ref[...].astype(BF16)
    for o in range(out_ref.shape[0]):
        out_ref[o] = table


def pack_rows(d_in, out_width, hidden, emb, item_rows):
    starts = [0, d_in, d_in + out_width // emb * hidden]
    starts.append(starts[-1] + -(-item_rows // 16) * 16)
    starts.append(starts[-1] + 16)
    return starts + [starts[-1] + 16]


def prep_kernel(at, w_ref, v_ref, items_ref, sizes_ref, bias_ref, out_ref):
    hidden, width = v_ref.shape
    emb = out_ref.shape[1]
    out_ref[at[0] : at[1], :] = w_ref[...]
    for j in range(width // emb):
        out_ref[at[1] + j * hidden : at[1] + (j + 1) * hidden, :] = v_ref[
            :, j * emb : (j + 1) * emb
        ]

    def padded(x, rows):
        if x.shape[0] == rows:
            return x
        return jnp.concatenate([x, jnp.zeros((rows - x.shape[0], emb), F32)], axis=0)

    items = items_ref[...].astype(F32)
    out_ref[at[2] : at[3], :] = padded(items, at[3] - at[2]).astype(BF16)
    out_ref[at[3] : at[4], :] = padded(sizes_ref[...].astype(F32), 16).astype(BF16)
    bias = bias_ref[...]
    hi = bias.astype(BF16).astype(F32)
    mid = (bias - hi).astype(BF16).astype(F32)
    low = bias - hi - mid
    out_ref[at[4] : at[5], :] = padded(jnp.concatenate([hi, mid, low], axis=0), 16).astype(BF16)


def place_kernel(mp_count, slots, map_ref, ids_ref, pos_ref):
    touch = ids_ref.shape[1]
    map_rows, lanes = map_ref.shape
    ids_col = column(ids_ref[...])
    in_row = (iota((touch, map_rows), 1) == ids_col // lanes).astype(F32)
    picked = lax.dot_general(
        in_row, map_ref[...].astype(F32), (((1,), (0,)), ((), ())),
        precision=lax.Precision.HIGHEST, preferred_element_type=F32,
    )
    in_lane = iota((touch, lanes), 1) == ids_col % lanes
    stored = jnp.sum(jnp.where(in_lane, picked, 0.0), axis=1, keepdims=True).astype(I32)
    stored = jnp.broadcast_to(stored, (touch, lanes))
    pos_ref[...] = stored // (mp_count * slots) * slots + stored % slots


def count_kernel(
    share, touch, at, item_rows, count_rows, p0, p1, cnt_ref, cntt_ref,
    items_ref, starts_ref, ends_ref, acc_ref,
):
    lanes = p0.shape[1]
    my = lax.axis_index("mp")
    per = share // lanes
    block = min(item_rows, -(-3 * item_rows // 8))
    sub_t = iota((touch, lanes), 0, F32)
    upto = (iota((lanes, lanes), 0) <= iota((lanes, lanes), 1)).astype(F32).astype(BF16)
    packs = (p0, p1)
    for k, pack in enumerate(packs):
        sizes = pack[at[3] : at[4], :]
        ends = dot(sizes, upto)[:count_rows]
        sizes = sizes.astype(F32)[:count_rows]
        totals = jnp.broadcast_to(jnp.sum(sizes, axis=1, keepdims=True), ends.shape)
        row = iota(ends.shape, 0)
        for r in range(count_rows - 1):
            ends = ends + jnp.where(row > r, totals[r : r + 1, :], 0.0)
        ends_ref[k] = ends
        starts_ref[k] = ends - sizes
        items_ref[k] = pack[at[2] : at[3], :].astype(F32)[:item_rows]

    def rows_of(ref, k):
        return jnp.concatenate([ref[k, pl.ds(my * per + j, 1), :] for j in range(per)], axis=1)

    bounds = []
    for k in range(len(packs)):
        starts = rows_of(starts_ref, k)
        ends = rows_of(ends_ref, k)
        first = jnp.min(starts).astype(I32) // lanes
        last = (jnp.max(ends).astype(I32) + lanes - 1) // lanes
        bounds.append((starts, ends, jnp.minimum(first, item_rows - block), last))

    def counted(k, first, rows, starts, ends):
        pick = jnp.concatenate(
            [
                (sub_t == items_ref[k, pl.ds(first + j, 1), :]).astype(F32).astype(BF16)
                for j in range(rows)
            ],
            axis=1,
        )
        pos = iota((rows * lanes, share), 0, F32) + (first * lanes).astype(F32)
        memb = ((pos >= starts) & (pos < ends)).astype(F32).astype(BF16)
        return dot(pick, memb)

    for k, (starts, ends, first, last) in enumerate(bounds):
        acc_ref[...] = counted(k, first, block, starts, ends)

        def body(c, carry):
            acc_ref[...] += counted(k, c, 1, starts, ends)
            return carry

        lax.fori_loop(first + block, last, body, 0)
        counts_t = acc_ref[...]
        cntt_ref[k * touch : (k + 1) * touch, :] = counts_t.astype(BF16)
        cnt_ref[:, k * touch : (k + 1) * touch] = counts_t.T.astype(BF16)


def pre_kernel(
    share, at, hidden, p0, p1, p2, p3, grads_ref, rows_ref, wt_ref, tail_ref, pre_ref, back_ref
):
    my = lax.axis_index("mp")
    emb = p0.shape[1]
    hot_cols = rows_ref.shape[0]
    grads = grads_ref[pl.ds(pl.multiple_of(my * share, share), share), :]
    rows = rows_ref[...]
    for k, p in enumerate((p0, p1, p2, p3)):
        cols = slice(k * hidden, (k + 1) * hidden)
        bias = jnp.sum(p[at[4] : at[5], :].astype(F32), axis=0, keepdims=True)
        pre_ref[:, cols] = dot(rows, p[:hot_cols, :], TN) + bias
        back = jnp.zeros((share, hidden), F32)
        for j in range(grads.shape[1] // emb):
            piece = p[at[1] + j * hidden : at[1] + (j + 1) * hidden, :]
            back = back + dot(grads[:, j * emb : (j + 1) * emb], piece, NT)
        back_ref[:, cols] = back
        tail_ref[:, cols] = p[hot_cols : at[1], :]
        wt_ref[cols, :] = p[: at[1], :].astype(F32).T.astype(BF16)


def fetch_kernel(pos_ref, table_ref, out_ref):
    owners, slots, _ = table_ref.shape

    def body(o, acc):
        return acc + dot(hits(pos_ref, o * slots, slots), table_ref[o])

    out_ref[...] = loop(owners, body, jnp.zeros(out_ref.shape, F32)).astype(BF16)


def fetch_near_kernel(pos_ref, *refs):
    out_ref = refs[-1]
    slots = refs[0].shape[0]
    my = lax.axis_index("dp")
    acc = jnp.zeros(out_ref.shape, F32)
    for k, table in enumerate(refs[:-1]):
        acc = acc + dot(hits(pos_ref, (my ^ k) * slots, slots), table[...])
    out_ref[...] = acc.astype(BF16)


def hits(pos_ref, first, slots):
    rel = pos_ref[...] - first
    lane = iota(rel.shape, 1)
    lanes = rel.shape[1]
    return jnp.concatenate(
        [(lane + j * lanes == rel).astype(F32).astype(BF16) for j in range(slots // lanes)], axis=1
    )


def onehot_kernel(
    share, fields, slots, cap, ids_ref, pos_ref, hot_ref, out_ref, q_ref, srow_ref, rows_ref
):
    my = lax.axis_index("mp")
    emb = hot_ref.shape[1]
    hot = hot_ref[...].T.astype(BF16)
    sub = iota((out_ref.shape[0], share), 0)
    for f in range(fields):
        mine = ids_ref[f : f + 1, pl.ds(pl.multiple_of(my * share, share), share)]
        hit = (sub == mine).astype(F32).astype(BF16)
        out_ref[:, f * share : (f + 1) * share] = hit
        rows_ref[f * emb : (f + 1) * emb, :] = dot(hot, hit).astype(BF16)
    pos = pos_ref[...]
    touch, lanes = pos.shape
    row = pos.T[0:1, :]
    owner = row // slots
    before = iota((touch, touch), 0) < iota((touch, touch), 1)
    rank = jnp.sum(
        ((pos[:, 0:1] // slots == owner) & before).astype(F32), axis=0, keepdims=True
    )
    bucket = owner.astype(F32) * float(cap) + rank
    q_ref[...] = (iota(q_ref.shape, 0, F32) == bucket).astype(F32).astype(BF16)
    at_rank = (iota((touch, lanes), 1, F32) == column(rank)).astype(F32)
    mine = jnp.where(
        iota((srow_ref.shape[0], touch), 0) // 8 == owner, (row % slots).astype(F32), 0.0
    )
    srow_ref[...] = lax.dot_general(
        mine, at_rank, (((1,), (0,)), ((), ())),
        precision=lax.Precision.HIGHEST, preferred_element_type=F32,
    )


def main_kernel(
    fields, cnta_ref, cntb_ref, f0, f1, f2, f3, pre_ref, back_ref, tail_ref, wt_ref, oht_ref,
    ig_ref, bag_ref, send_ref,
):
    touch, emb = f0.shape
    share = cnta_ref.shape[0]
    core = lax.axis_index("mp") % 2
    pooled = jnp.zeros((share, emb), F32)
    for k, f in enumerate((f0, f1, f2, f3)):
        cnt = (cnta_ref, cntb_ref)[k // 2]
        pooled = pooled + dot(cnt[:, k % 2 * touch : (k % 2 + 1) * touch], f[...])
    pre = pre_ref[...] + dot(pooled.astype(BF16), tail_ref[...])
    sig = jax.nn.sigmoid(pre)
    hidden = (back_ref[...] * sig * (1.0 + pre * (1.0 - sig))).astype(BF16)
    grad = dot(hidden, wt_ref[...])
    for f in range(fields):
        ig_ref[f * share : (f + 1) * share, :] = hi_lo(grad[:, f * emb : (f + 1) * emb])
    bag_ref[...] = hi_lo(grad[:, fields * emb :])
    half = send_ref.shape[0]
    first = pl.multiple_of((1 - core) * half, half)
    send_ref[...] = sum_halves(dot(oht_ref[pl.ds(first, half), :], ig_ref[...]))


def keep_kernel(oht_ref, ig_ref, bag_ref, cntta_ref, cnttb_ref, keep_ref, touch_send, touch_keep):
    half = keep_ref.shape[0]
    core = lax.axis_index("mp") % 2
    first = pl.multiple_of(core * half, half)
    keep_ref[...] = sum_halves(dot(oht_ref[pl.ds(first, half), :], ig_ref[...]))
    touch = touch_send.shape[1]
    for k in range(4):
        ref = touch_send if k % 2 else touch_keep
        counts = (cntta_ref, cnttb_ref)[k // 2]
        rows = slice(k % 2 * touch, (k % 2 + 1) * touch)
        ref[k // 2] = sum_halves(dot(counts[rows, :], bag_ref[...]))


def add_kernel(a_ref, b_ref, out_ref):
    out_ref[...] = a_ref[...] + b_ref[...]


def pair_kernel(keep_ref, got_ref, mine_ref, give_ref):
    mine_ref[...] = keep_ref[0] + got_ref[0]
    give_ref[...] = keep_ref[1] + got_ref[1]


def fetch_kernel(pos_ref, table_ref, out_ref):
    owners, slots, emb = table_ref.shape
    touch, lanes = pos_ref.shape
    lane = iota((touch, lanes), 1)

    def body(o, acc):
        rel = pos_ref[...] - o * slots
        hit = jnp.concatenate(
            [
                (lane + j * lanes == rel).astype(F32).astype(BF16)
                for j in range(slots // lanes)
            ],
            axis=1,
        )
        return acc + dot(hit, table_ref[o])

    out_ref[...] = loop(owners, body, jnp.zeros((touch, emb), F32)).astype(BF16)


def reduce_kernel(parts_ref, out_ref):
    total = jnp.sum(parts_ref[...], axis=0, keepdims=True)
    out_ref[...] = jnp.broadcast_to(total, out_ref.shape)


def near_place(far, k):
    near = lax.axis_index("dp") % 2
    group = lax.axis_index("mp") // 2
    return (far * 2 + (near ^ (k // 2))) * 2 + (group ^ (k % 2))


def split_near_kernel(keep_ref, got_ref, *outs):
    for k, ref in enumerate(outs):
        for far in range(ref.shape[0]):
            at = near_place(far, k)
            ref[far] = keep_ref[at] + got_ref[at]


def sum_kernel(a_ref, b_ref, c_ref, d_ref, out_ref):
    out_ref[...] = (a_ref[...] + b_ref[...]) + (c_ref[...] + d_ref[...])


def order_near_kernel(*refs):
    for k, ref in enumerate(refs[:-1]):
        for far in range(ref.shape[0]):
            refs[-1][near_place(far, k)] = ref[far]


def pack_kernel(cap, mine_ref, got_ref, q_ref, srow_ref, out_ref):
    owners = out_ref.shape[0]
    emb = out_ref.shape[2]
    rows = sum_halves(dot(q_ref[...], hi_lo(mine_ref[...] + got_ref[...])))
    out_ref[:, :cap, :] = rows.reshape(owners, cap, emb)
    out_ref[:, cap:, :] = srow_ref[...].reshape(owners, 8, emb)


def cold_kernel(cap, arrived_ref, table_ref, accum_ref, new_ref, acc_ref):
    slots, emb = table_ref.shape
    sub = iota((slots, cap), 0, F32)

    def body(d, acc):
        slot = arrived_ref[d, cap : cap + 1, :][:, :cap]
        hit = (sub == slot).astype(F32).astype(BF16)
        return acc + dot(hit, hi_lo(arrived_ref[d, :cap, :]))

    grad = sum_halves(loop(arrived_ref.shape[0], body, jnp.zeros((slots, 2 * emb), F32)))
    new_ref[...], acc_ref[...] = adagrad(table_ref[...], accum_ref[...], grad)


def final_kernel(mine_ref, theirs_ref, table_ref, accum_ref, new_ref, acc_ref):
    half = mine_ref.shape[0]
    core = lax.axis_index("mp") % 2
    for ref, c in ((mine_ref, core), (theirs_ref, 1 - core)):
        at = pl.ds(pl.multiple_of(c * half, half), half)
        new_ref[at, :], acc_ref[at, :] = adagrad(table_ref[at, :], accum_ref[at, :], ref[...])


def per_device(
    hot_ids,
    touched,
    cold_items,
    bag_counts,
    owner_map,
    grad_out,
    weight_in,
    bias_in,
    weight_out,
    hot_table,
    hot_accum,
    cold_table,
    cold_accum,
):
    dp_count = lax.axis_size("dp")
    mp_count = lax.axis_size("mp")
    slots, emb = cold_table.shape
    samples, fields = hot_ids.shape
    touch = touched.shape[2]
    items = cold_items.shape[2]
    d_in, hidden = weight_in.shape
    all_hidden = mp_count * hidden
    hot_rows = hot_table.shape[0]
    share = samples // mp_count
    cap = -(-(2 * touch // dp_count) // 8) * 8
    item_rows = items // emb
    count_rows = samples // emb
    both = ("dp", "mp")

    def swap(x, mask):
        return lax.ppermute(x, "mp", [(i, i ^ mask) for i in range(mp_count)])

    def far_swap(x, mask):
        return lax.ppermute(x, "dp", [(i, i ^ mask) for i in range(dp_count)])

    near = dp_count == 8 and mp_count == 4

    if near:
        (own,) = call(cast_kernel, [((slots, emb), BF16, True)], [cold_table], late=(0,))
        tables = [own] + [None] * 7
        for k in (4, 6, 2):
            tables[k] = far_swap(own, k)
        for k in (0, 4, 6, 2):
            tables[k + 1] = far_swap(tables[k], 1)
    else:
        (mine,) = call(
            spread_kernel, [((dp_count, slots, emb), BF16, False)], [cold_table], late=(0,)
        )
        tables = [lax.all_to_all(mine, "dp", split_axis=0, concat_axis=0, tiled=True)]

    at = pack_rows(d_in, weight_out.shape[1], hidden, emb, item_rows)
    (pack,) = call(
        lambda *r: prep_kernel(at, *r),
        [((at[-1], emb), BF16, True)],
        [
            weight_in,
            weight_out,
            cold_items.reshape(item_rows, emb),
            bag_counts.reshape(count_rows, emb),
            bias_in.reshape(1, hidden),
        ],
        late=range(5),
    )
    pack_far = swap(pack, 2)
    pack_near = swap(pack, 1)
    pack_cross = swap(pack_far, 1)
    packs = [pack, pack_near, pack_far, pack_cross]

    (pos,) = call(
        lambda *r: place_kernel(mp_count, slots, *r),
        [((touch, emb), I32, True)],
        [owner_map.reshape(-1, emb), touched.reshape(1, touch)],
        late=range(2),
    )

    def count(pair):
        return call(
            lambda *r: count_kernel(share, touch, at, item_rows, count_rows, *r),
            [((share, 2 * touch), BF16, True), ((2 * touch, share), BF16, True)],
            pair,
            scratch=[
                pltpu.VMEM((2, item_rows, emb), F32),
                pltpu.VMEM((2, count_rows, emb), F32),
                pltpu.VMEM((2, count_rows, emb), F32),
                pltpu.VMEM((touch, share), F32),
            ],
        )

    cnta, cntta = count(packs[:2])
    cntb, cnttb = count(packs[2:])

    oht, q_mat, slot_rows, rows = call(
        lambda *r: onehot_kernel(share, fields, slots, cap, *r),
        [
            ((hot_rows, fields * share), BF16, True),
            ((dp_count * cap, touch), BF16, True),
            ((dp_count * 8, emb), F32, True),
            ((fields * emb, share), BF16, True),
        ],
        [hot_ids.T, pos, hot_table],
        late=(0, 2),
    )

    wt, tail, pre, back = call(
        lambda *r: pre_kernel(share, at, hidden, *r),
        [
            ((all_hidden, d_in), BF16, True),
            ((emb, all_hidden), BF16, True),
            ((share, all_hidden), F32, True),
            ((share, all_hidden), F32, True),
        ],
        [*packs, grad_out, rows],
        late=(4,),
    )

    (fetched,) = call(
        fetch_near_kernel if near else fetch_kernel,
        [((touch, emb), BF16, True)],
        [pos, *tables],
        late=() if near else (1,),
    )
    far = swap(fetched, 2)
    around = [fetched, swap(fetched, 1), far, swap(far, 1)]

    half_rows = hot_rows // 2
    ig, bag, hot_send = call(
        lambda *r: main_kernel(fields, *r),
        [
            ((fields * share, 2 * emb), BF16, True),
            ((share, 2 * emb), BF16, True),
            ((half_rows, emb), F32, True),
        ],
        [cnta, cntb, *around, pre, back, tail, wt, oht],
    )
    hot_got = swap(hot_send, 1)
    hot_keep, touch_send, touch_keep = call(
        keep_kernel,
        [
            ((half_rows, emb), F32, True),
            ((mp_count // 2, touch, emb), F32, True),
            ((mp_count // 2, touch, emb), F32, True),
        ],
        [oht, ig, bag, cntta, cnttb],
    )

    group_size = dp_count * mp_count // 2
    rank_groups = [[g * 2 + c for g in range(group_size)] for c in range(2)]

    def exchange(x):
        return lax.all_to_all(
            x, both, split_axis=0, concat_axis=0, tiled=True, axis_index_groups=rank_groups
        )

    def near_swap(x, k):
        mask = k // 2 * mp_count + k % 2 * 2
        return lax.ppermute(
            x, both, [(i, i ^ mask) for i in range(dp_count * mp_count)]
        )

    if near:
        rows_each = half_rows // group_size
        shape = (group_size, rows_each, emb)
        line = (dp_count // 2, rows_each, emb)
        pieces = call(
            split_near_kernel,
            [(line, F32, True)] * 4,
            [hot_keep.reshape(shape), hot_got.reshape(shape)],
        )
        pieces = [near_swap(x, k) if k else x for k, x in enumerate(pieces)]
        (part,) = call(sum_kernel, [(line, F32, True)], pieces)
        pieces = [far_swap(part, 2 * k) if k else part for k in range(4)]
        (part,) = call(sum_kernel, [(line, F32, True)], pieces)
        pieces = [near_swap(part, k) if k else part for k in range(4)]
        (half,) = call(order_near_kernel, [(shape, F32, True)], pieces)
        half = half.reshape(half_rows, emb)
    else:
        (chip,) = call(add_kernel, [((half_rows, emb), F32, True)], [hot_keep, hot_got])
        parts = exchange(chip.reshape(group_size, -1, emb))
        (shard,) = call(reduce_kernel, [(parts.shape, F32, True)], [parts])
        half = exchange(shard).reshape(half_rows, emb)
    other = swap(half, 1)
    hot_updated, hot_accum_new = call(
        final_kernel, [(hot_table.shape, F32, False)] * 2, [half, other, hot_table, hot_accum]
    )

    touch_got = swap(touch_send, 1)
    mine, give = call(pair_kernel, [((touch, emb), F32, True)] * 2, [touch_keep, touch_got])
    got = swap(give, 2)
    (outgoing,) = call(
        lambda *r: pack_kernel(cap, *r),
        [((dp_count, cap + 8, emb), F32, True)],
        [mine, got, q_mat, slot_rows],
    )
    arrived = lax.all_to_all(outgoing, "dp", split_axis=0, concat_axis=0, tiled=True)
    cold_updated, cold_accum_new = call(
        lambda *r: cold_kernel(cap, *r),
        [(cold_table.shape, F32, False)] * 2,
        [arrived, cold_table, cold_accum],
    )
    return (hot_updated, hot_accum_new, cold_updated, cold_accum_new)


def solution(mesh):
    return whole(mesh)


def whole(mesh):
    return jax.shard_map(
        per_device,
        mesh=mesh,
        in_specs=(
            P("dp", None),
            P("dp", "mp", None),
            P("dp", "mp", None),
            P("dp", "mp", None),
            P(),
            P("dp", None),
            P(None, "mp"),
            P("mp"),
            P("mp", None),
            P(),
            P(),
            P(("dp", "mp"), None),
            P(("dp", "mp"), None),
        ),
        out_specs=(P(), P(), P(("dp", "mp"), None), P(("dp", "mp"), None)),
        check_vma=False,
    )
```

```python
import jax
import jax.numpy as jnp
from jax import lax
from jax.experimental import pallas as pl
from jax.experimental.pallas import tpu as pltpu
from jax.sharding import PartitionSpec as P

STEP_SIZE = 0.5
F32 = jnp.float32
BF16 = jnp.bfloat16
I32 = jnp.int32


def adagrad(table_rows, accum_rows, grad_rows):
    accum_new = accum_rows + grad_rows * grad_rows
    return (table_rows - STEP_SIZE * grad_rows / jnp.sqrt(accum_new), accum_new)


def loop(count, body, init):
    if count <= 16:
        for i in range(count):
            init = body(i, init)
        return init
    return lax.fori_loop(0, count, body, init)


def hi_lo(x):
    hi = x.astype(BF16)
    lo = (x - hi.astype(F32)).astype(BF16)
    return jnp.concatenate([hi, lo], axis=1)


def sum_halves(x):
    half = x.shape[1] // 2
    return x[:, :half] + x[:, half:]


def dot(a, b, dims=(((1,), (0,)), ((), ()))):
    return lax.dot_general(a, b, dims, preferred_element_type=F32)


NT = (((1,), (1,)), ((), ()))
TN = (((0,), (0,)), ((), ()))


def iota(shape, dim, dtype=I32):
    r = lax.broadcasted_iota(I32, shape, dim)
    return r if dtype == I32 else r.astype(dtype)


VM = pl.BlockSpec(memory_space=pltpu.VMEM)
ANY = pl.BlockSpec(memory_space=pl.ANY)


def call(body, outs, ins, scratch=(), late=(), raw=()):
    avals = [
        pltpu.VMEM(shape, dtype) if stay else jax.ShapeDtypeStruct(shape, dtype)
        for shape, dtype, stay in outs
    ]
    return pl.pallas_call(
        body,
        out_shape=avals,
        in_specs=[ANY if i in raw else VM for i in range(len(ins))],
        out_specs=[VM] * len(outs),
        scratch_shapes=scratch,
        compiler_params=pltpu.CompilerParams(vmem_limit_bytes=16 * 1024 * 1024),
    )(
        *[
            pltpu.with_memory_space_constraint(
                x, pltpu.HBM if i in late or i in raw else pltpu.VMEM
            )
            for i, x in enumerate(ins)
        ]
    )


def column(row):
    return jnp.broadcast_to(row, (8, row.shape[1])).T[:, 0:1]


def cast_kernel(count, *refs):
    sources, outs = refs[:count], refs[count : 2 * count]
    table_ref, sems = refs[2 * count :]
    copies = [
        pltpu.make_async_copy(src, outs[i] if i else table_ref, sems.at[i])
        for i, src in enumerate(sources)
    ]
    for copy in copies:
        copy.start()
    copies[0].wait()
    table = table_ref[...].astype(BF16)
    if len(outs[0].shape) == 2:
        outs[0][...] = table
    else:
        for o in range(outs[0].shape[0]):
            outs[0][o] = table
    for copy in copies[1:]:
        copy.wait()


def pack_rows(out_width, hidden, emb, item_rows):
    starts = [0, out_width // emb * hidden]
    starts.append(starts[-1] + -(-item_rows // 16) * 16)
    starts.append(starts[-1] + 16)
    return starts + [starts[-1] + 16]


def prep_kernel(at, v_ref, items_ref, sizes_ref, bias_ref, out_ref):
    hidden, width = v_ref.shape
    emb = out_ref.shape[1]
    for j in range(width // emb):
        out_ref[j * hidden : (j + 1) * hidden, :] = v_ref[:, j * emb : (j + 1) * emb]

    def padded(x, rows):
        if x.shape[0] == rows:
            return x
        return jnp.concatenate([x, jnp.zeros((rows - x.shape[0], emb), F32)], axis=0)

    items = items_ref[...].astype(F32)
    out_ref[at[1] : at[2], :] = padded(items, at[2] - at[1]).astype(BF16)
    out_ref[at[2] : at[3], :] = padded(sizes_ref[...].astype(F32), 16).astype(BF16)
    bias = bias_ref[...]
    hi = bias.astype(BF16).astype(F32)
    mid = (bias - hi).astype(BF16).astype(F32)
    low = bias - hi - mid
    out_ref[at[3] : at[4], :] = padded(jnp.concatenate([hi, mid, low], axis=0), 16).astype(BF16)


def place_kernel(
    mp_count, slots, share, map_ref, ids_ref, hot_hbm, hot_ids_hbm, weight_hbm, grads_hbm,
    pos_ref, row_ref, hot_ref, hot_ids_ref, weight_ref, grads_ref, sems,
):
    my = lax.axis_index("mp")
    mine = grads_hbm.at[pl.ds(pl.multiple_of(my * share, share), share), :]
    copies = [
        pltpu.make_async_copy(hot_hbm, hot_ref, sems.at[0]),
        pltpu.make_async_copy(hot_ids_hbm, hot_ids_ref, sems.at[1]),
        pltpu.make_async_copy(weight_hbm, weight_ref, sems.at[2]),
        pltpu.make_async_copy(mine, grads_ref, sems.at[3]),
    ]
    for copy in copies:
        copy.start()
    touch = ids_ref.shape[1]
    map_rows, lanes = map_ref.shape
    ids_col = column(ids_ref[...])
    in_row = (iota((touch, map_rows), 1) == ids_col // lanes).astype(F32)
    picked = lax.dot_general(
        in_row, map_ref[...].astype(F32), (((1,), (0,)), ((), ())),
        precision=lax.Precision.HIGHEST, preferred_element_type=F32,
    )
    in_lane = iota((touch, lanes), 1) == ids_col % lanes
    stored = jnp.sum(jnp.where(in_lane, picked, 0.0), axis=1, keepdims=True).astype(I32)
    stored = jnp.broadcast_to(stored, (touch, lanes))
    pos = stored // (mp_count * slots) * slots + stored % slots
    pos_ref[...] = pos
    row_ref[...] = pos.T[:8, :]
    for copy in copies:
        copy.wait()


def count_kernel(
    share, touch, at, item_rows, count_rows, p0, p1, cnt_ref, cntt_ref,
    items_ref, starts_ref, ends_ref, acc_ref,
):
    lanes = p0.shape[1]
    my = lax.axis_index("mp")
    per = share // lanes
    block = min(item_rows, -(-3 * item_rows // 8))
    sub_t = iota((touch, lanes), 0, F32)
    upto = (iota((lanes, lanes), 0) <= iota((lanes, lanes), 1)).astype(F32).astype(BF16)
    packs = (p0, p1)
    for k, pack in enumerate(packs):
        sizes = pack[at[2] : at[3], :]
        ends = dot(sizes, upto)[:count_rows]
        sizes = sizes.astype(F32)[:count_rows]
        totals = jnp.broadcast_to(jnp.sum(sizes, axis=1, keepdims=True), ends.shape)
        row = iota(ends.shape, 0)
        for r in range(count_rows - 1):
            ends = ends + jnp.where(row > r, totals[r : r + 1, :], 0.0)
        ends_ref[k] = ends
        starts_ref[k] = ends - sizes
        items_ref[k] = pack[at[1] : at[2], :].astype(F32)[:item_rows]

    def rows_of(ref, k):
        return jnp.concatenate([ref[k, pl.ds(my * per + j, 1), :] for j in range(per)], axis=1)

    bounds = []
    for k in range(len(packs)):
        starts = rows_of(starts_ref, k)
        ends = rows_of(ends_ref, k)
        first = jnp.min(starts).astype(I32) // lanes
        last = (jnp.max(ends).astype(I32) + lanes - 1) // lanes
        bounds.append((starts, ends, jnp.minimum(first, item_rows - block), last))

    def counted(k, first, rows, starts, ends):
        pick = jnp.concatenate(
            [
                (sub_t == items_ref[k, pl.ds(first + j, 1), :]).astype(F32).astype(BF16)
                for j in range(rows)
            ],
            axis=1,
        )
        pos = iota((rows * lanes, share), 0, F32) + (first * lanes).astype(F32)
        memb = ((pos >= starts) & (pos < ends)).astype(F32).astype(BF16)
        return dot(pick, memb)

    for k, (starts, ends, first, last) in enumerate(bounds):
        acc_ref[...] = counted(k, first, block, starts, ends)

        def body(c, carry):
            acc_ref[...] += counted(k, c, 1, starts, ends)
            return carry

        lax.fori_loop(first + block, last, body, 0)
        counts_t = acc_ref[...]
        cntt_ref[k * touch : (k + 1) * touch, :] = counts_t.astype(BF16)
        cnt_ref[:, k * touch : (k + 1) * touch] = counts_t.T.astype(BF16)


def pre_kernel(
    share, at, hidden, w0, w1, w2, w3, p0, p1, p2, p3, grads_ref, rows_ref,
    wt_ref, tail_ref, pre_ref, back_ref,
):
    emb = p0.shape[1]
    hot_cols = rows_ref.shape[0]
    grads = grads_ref[...]
    rows = rows_ref[...]
    for k, (w, p) in enumerate(zip((w0, w1, w2, w3), (p0, p1, p2, p3))):
        cols = slice(k * hidden, (k + 1) * hidden)
        bias = jnp.sum(p[at[3] : at[4], :].astype(F32), axis=0, keepdims=True)
        pre_ref[:, cols] = dot(rows, w[:hot_cols, :], TN) + bias
        back = jnp.zeros((share, hidden), F32)
        for j in range(grads.shape[1] // emb):
            piece = p[j * hidden : (j + 1) * hidden, :]
            back = back + dot(grads[:, j * emb : (j + 1) * emb], piece, NT)
        back_ref[:, cols] = back
        tail_ref[:, cols] = w[hot_cols:, :]
        wt_ref[cols, :] = w[...].astype(F32).T.astype(BF16)


def fetch_kernel(pos_ref, table_ref, out_ref):
    owners, slots, _ = table_ref.shape

    def body(o, acc):
        return acc + dot(hits(pos_ref[...], o * slots, slots), table_ref[o])

    out_ref[...] = loop(owners, body, jnp.zeros(out_ref.shape, F32)).astype(BF16)


def fetch_near_kernel(pos_ref, row_ref, *refs):
    tables, (mine_ref, give_ref) = refs[:-2], refs[-2:]
    touch, lanes = pos_ref.shape
    slots = tables[0].shape[0]
    my = lax.axis_index("dp")
    theirs = jnp.broadcast_to(row_ref[...].T[:, 0:1], (touch, lanes))
    both = jnp.concatenate([pos_ref[...], theirs], axis=0)
    acc = jnp.zeros((2 * touch, mine_ref.shape[1]), F32)
    for k, table in enumerate(tables):
        acc = acc + dot(hits(both, (my ^ (2 * k)) * slots, slots), table[...])
    mine_ref[...] = acc[:touch].astype(BF16)
    give_ref[...] = acc[touch:].astype(BF16)


def join_kernel(mine_ref, near_ref, far_ref, cross_ref, out_ref):
    out_ref[0] = (mine_ref[...].astype(F32) + near_ref[...].astype(F32)).astype(BF16)
    out_ref[1] = (far_ref[...].astype(F32) + cross_ref[...].astype(F32)).astype(BF16)


def hits(pos, first, slots):
    rel = pos - first
    lane = iota(rel.shape, 1)
    lanes = rel.shape[1]
    return jnp.concatenate(
        [(lane + j * lanes == rel).astype(F32).astype(BF16) for j in range(slots // lanes)], axis=1
    )


def onehot_kernel(share, fields, ids_ref, hot_ref, out_ref, rows_ref):
    my = lax.axis_index("mp")
    emb = hot_ref.shape[1]
    hot = hot_ref[...].T.astype(BF16)
    sub = iota((out_ref.shape[0], share), 0)
    for f in range(fields):
        mine = ids_ref[f : f + 1, pl.ds(pl.multiple_of(my * share, share), share)]
        hit = (sub == mine).astype(F32).astype(BF16)
        out_ref[:, f * share : (f + 1) * share] = hit
        rows_ref[f * emb : (f + 1) * emb, :] = dot(hot, hit).astype(BF16)


def bucket_kernel(slots, cap, pos_ref, q_ref, srow_ref):
    pos = pos_ref[...]
    touch, lanes = pos.shape
    row = pos.T[0:1, :]
    owner = row // slots
    before = iota((touch, touch), 0) < iota((touch, touch), 1)
    rank = jnp.sum(
        ((pos[:, 0:1] // slots == owner) & before).astype(F32), axis=0, keepdims=True
    )
    bucket = owner.astype(F32) * float(cap) + rank
    q_ref[...] = (iota(q_ref.shape, 0, F32) == bucket).astype(F32).astype(BF16)
    at_rank = (iota((touch, lanes), 1, F32) == column(rank)).astype(F32)
    mine = jnp.where(
        iota((srow_ref.shape[0], touch), 0) // 8 == owner, (row % slots).astype(F32), 0.0
    )
    srow_ref[...] = lax.dot_general(
        mine, at_rank, (((1,), (0,)), ((), ())),
        precision=lax.Precision.HIGHEST, preferred_element_type=F32,
    )


def main_kernel(
    fields, cnta_ref, cntb_ref, mine_ref, core_ref, pre_ref, back_ref, tail_ref, wt_ref, oht_ref,
    ig_ref, bag_ref, send_ref,
):
    _, touch, emb = mine_ref.shape
    share = cnta_ref.shape[0]
    core = lax.axis_index("mp") % 2
    pooled = jnp.zeros((share, emb), F32)
    for k in range(4):
        cnt = (cnta_ref, cntb_ref)[k // 2]
        rows = (mine_ref, core_ref)[k % 2][k // 2]
        pooled = pooled + dot(cnt[:, k % 2 * touch : (k % 2 + 1) * touch], rows)
    pre = pre_ref[...] + dot(pooled.astype(BF16), tail_ref[...])
    sig = jax.nn.sigmoid(pre)
    hidden = (back_ref[...] * sig * (1.0 + pre * (1.0 - sig))).astype(BF16)
    grad = dot(hidden, wt_ref[...])
    for f in range(fields):
        ig_ref[f * share : (f + 1) * share, :] = hi_lo(grad[:, f * emb : (f + 1) * emb])
    bag_ref[...] = hi_lo(grad[:, fields * emb :])
    half = send_ref.shape[0]
    first = pl.multiple_of((1 - core) * half, half)
    send_ref[...] = sum_halves(dot(oht_ref[pl.ds(first, half), :], ig_ref[...]))


def keep_kernel(oht_ref, ig_ref, bag_ref, cntta_ref, cnttb_ref, keep_ref, touch_send, touch_keep):
    half = keep_ref.shape[0]
    core = lax.axis_index("mp") % 2
    first = pl.multiple_of(core * half, half)
    keep_ref[...] = sum_halves(dot(oht_ref[pl.ds(first, half), :], ig_ref[...]))
    touch = touch_send.shape[1]
    for k in range(4):
        ref = touch_send if k % 2 else touch_keep
        counts = (cntta_ref, cnttb_ref)[k // 2]
        rows = slice(k % 2 * touch, (k % 2 + 1) * touch)
        ref[k // 2] = sum_halves(dot(counts[rows, :], bag_ref[...]))


def add_kernel(a_ref, b_ref, out_ref):
    out_ref[...] = a_ref[...] + b_ref[...]


def pair_kernel(keep_ref, got_ref, mine_ref, give_ref):
    mine_ref[...] = keep_ref[0] + got_ref[0]
    give_ref[...] = keep_ref[1] + got_ref[1]


def fetch_kernel(pos_ref, table_ref, out_ref):
    owners, slots, emb = table_ref.shape
    touch, lanes = pos_ref.shape
    lane = iota((touch, lanes), 1)

    def body(o, acc):
        rel = pos_ref[...] - o * slots
        hit = jnp.concatenate(
            [
                (lane + j * lanes == rel).astype(F32).astype(BF16)
                for j in range(slots // lanes)
            ],
            axis=1,
        )
        return acc + dot(hit, table_ref[o])

    out_ref[...] = loop(owners, body, jnp.zeros((touch, emb), F32)).astype(BF16)


def reduce_kernel(parts_ref, out_ref):
    total = jnp.sum(parts_ref[...], axis=0, keepdims=True)
    out_ref[...] = jnp.broadcast_to(total, out_ref.shape)


def near_place(far, k):
    near = lax.axis_index("dp") % 2
    group = lax.axis_index("mp") // 2
    return (far * 2 + (near ^ (k // 2))) * 2 + (group ^ (k % 2))


def split_near_kernel(keep_ref, got_ref, *outs):
    for k, ref in enumerate(outs):
        for far in range(ref.shape[0]):
            at = near_place(far, k)
            ref[far] = keep_ref[at] + got_ref[at]


def sum_kernel(a_ref, b_ref, c_ref, d_ref, out_ref):
    out_ref[...] = (a_ref[...] + b_ref[...]) + (c_ref[...] + d_ref[...])


def order_near_kernel(*refs):
    for k, ref in enumerate(refs[:-1]):
        for far in range(ref.shape[0]):
            refs[-1][near_place(far, k)] = ref[far]


def pack_kernel(cap, mine_ref, got_ref, q_ref, srow_ref, out_ref):
    owners = out_ref.shape[0]
    emb = out_ref.shape[2]
    rows = sum_halves(dot(q_ref[...], hi_lo(mine_ref[...] + got_ref[...])))
    out_ref[:, :cap, :] = rows.reshape(owners, cap, emb)
    out_ref[:, cap:, :] = srow_ref[...].reshape(owners, 8, emb)


def cold_kernel(cap, arrived_ref, table_ref, accum_ref, new_ref, acc_ref):
    slots, emb = table_ref.shape
    sub = iota((slots, cap), 0, F32)

    def body(d, acc):
        slot = arrived_ref[d, cap : cap + 1, :][:, :cap]
        hit = (sub == slot).astype(F32).astype(BF16)
        return acc + dot(hit, hi_lo(arrived_ref[d, :cap, :]))

    grad = sum_halves(loop(arrived_ref.shape[0], body, jnp.zeros((slots, 2 * emb), F32)))
    new_ref[...], acc_ref[...] = adagrad(table_ref[...], accum_ref[...], grad)


def final_kernel(mine_ref, theirs_ref, table_ref, accum_ref, new_ref, acc_ref):
    half = mine_ref.shape[0]
    core = lax.axis_index("mp") % 2
    for ref, c in ((mine_ref, core), (theirs_ref, 1 - core)):
        at = pl.ds(pl.multiple_of(c * half, half), half)
        new_ref[at, :], acc_ref[at, :] = adagrad(table_ref[at, :], accum_ref[at, :], ref[...])


def per_device(
    hot_ids,
    touched,
    cold_items,
    bag_counts,
    owner_map,
    grad_out,
    weight_in,
    bias_in,
    weight_out,
    hot_table,
    hot_accum,
    cold_table,
    cold_accum,
):
    dp_count = lax.axis_size("dp")
    mp_count = lax.axis_size("mp")
    slots, emb = cold_table.shape
    samples, fields = hot_ids.shape
    touch = touched.shape[2]
    items = cold_items.shape[2]
    d_in, hidden = weight_in.shape
    all_hidden = mp_count * hidden
    hot_rows = hot_table.shape[0]
    share = samples // mp_count
    cap = -(-(2 * touch // dp_count) // 8) * 8
    item_rows = items // emb
    count_rows = samples // emb
    both = ("dp", "mp")

    def swap(x, mask):
        return lax.ppermute(x, "mp", [(i, i ^ mask) for i in range(mp_count)])

    def far_swap(x, mask):
        return lax.ppermute(x, "dp", [(i, i ^ mask) for i in range(dp_count)])

    def near_swap(x, k):
        mask = k // 2 * mp_count + k % 2 * 2
        return lax.ppermute(
            x, both, [(i, i ^ mask) for i in range(dp_count * mp_count)]
        )

    near = dp_count == 8 and mp_count == 4

    small = [
        owner_map.reshape(-1, emb),
        touched.reshape(1, touch),
        weight_out,
        cold_items.reshape(item_rows, emb),
        bag_counts.reshape(count_rows, emb),
        bias_in.reshape(1, hidden),
    ]
    own, *small = call(
        lambda *r: cast_kernel(1 + len(small), *r),
        [((slots, emb) if near else (dp_count, slots, emb), BF16, near)]
        + [(x.shape, x.dtype, True) for x in small],
        [cold_table, *small],
        raw=range(1 + len(small)),
        scratch=[
            pltpu.VMEM((slots, emb), F32),
            pltpu.SemaphoreType.DMA((1 + len(small),)),
        ],
    )
    map_rows, touched_row, *small = small
    if near:
        tables = [own]
        for k in (2, 4, 6):
            tables.append(far_swap(own, k))
    else:
        tables = lax.all_to_all(own, "dp", split_axis=0, concat_axis=0, tiled=True)

    w_far = swap(weight_in, 2)
    w_near = swap(weight_in, 1)
    weights = [weight_in, w_near, w_far, swap(w_far, 1)]
    at = pack_rows(weight_out.shape[1], hidden, emb, item_rows)
    (pack,) = call(lambda *r: prep_kernel(at, *r), [((at[-1], emb), BF16, True)], small)
    pack_far = swap(pack, 2)
    pack_near = swap(pack, 1)
    packs = [pack, pack_near, pack_far, swap(pack_far, 1)]

    pos, pos_row, hot_near, ids_near, weight_near, grads_near = call(
        lambda *r: place_kernel(mp_count, slots, share, *r),
        [
            ((touch, emb), I32, True),
            ((8, touch), I32, True),
            (hot_table.shape, F32, True),
            ((fields, samples), I32, True),
            (weight_in.shape, BF16, True),
            ((share, grad_out.shape[1]), BF16, True),
        ],
        [map_rows, touched_row, hot_table, hot_ids.T, weight_in, grad_out],
        raw=range(2, 6),
        scratch=[pltpu.SemaphoreType.DMA((4,))],
    )
    weights[0] = weight_near

    def count(pair):
        return call(
            lambda *r: count_kernel(share, touch, at, item_rows, count_rows, *r),
            [((share, 2 * touch), BF16, True), ((2 * touch, share), BF16, True)],
            pair,
            scratch=[
                pltpu.VMEM((2, item_rows, emb), F32),
                pltpu.VMEM((2, count_rows, emb), F32),
                pltpu.VMEM((2, count_rows, emb), F32),
                pltpu.VMEM((touch, share), F32),
            ],
        )

    cnta, cntta = count(packs[:2])
    cntb, cnttb = count(packs[2:])

    oht, rows = call(
        lambda *r: onehot_kernel(share, fields, *r),
        [((hot_rows, fields * share), BF16, True), ((fields * emb, share), BF16, True)],
        [ids_near, hot_near],
    )

    wt, tail, pre, back = call(
        lambda *r: pre_kernel(share, at, hidden, *r),
        [
            ((all_hidden, d_in), BF16, True),
            ((emb, all_hidden), BF16, True),
            ((share, all_hidden), F32, True),
            ((share, all_hidden), F32, True),
        ],
        [*weights, *packs, grads_near, rows],
    )

    if near:
        other_row = far_swap(pos_row, 1)
        mine, give = call(
            fetch_near_kernel, [((touch, emb), BF16, True)] * 2, [pos, other_row, *tables]
        )
        from_near = near_swap(give, 2)
        from_far = near_swap(mine, 1)
        from_cross = near_swap(give, 3)
        (fetched,) = call(
            join_kernel, [((2, touch, emb), BF16, True)], [mine, from_near, from_far, from_cross]
        )
    else:
        (mine,) = call(fetch_kernel, [((touch, emb), BF16, True)], [pos, tables], late=(1,))
        fetched = jnp.stack([mine, swap(mine, 2)])
    fetched_core = swap(fetched, 1)

    half_rows = hot_rows // 2
    ig, bag, hot_send = call(
        lambda *r: main_kernel(fields, *r),
        [
            ((fields * share, 2 * emb), BF16, True),
            ((share, 2 * emb), BF16, True),
            ((half_rows, emb), F32, True),
        ],
        [cnta, cntb, fetched, fetched_core, pre, back, tail, wt, oht],
    )
    hot_got = swap(hot_send, 1)
    hot_keep, touch_send, touch_keep = call(
        keep_kernel,
        [
            ((half_rows, emb), F32, True),
            ((mp_count // 2, touch, emb), F32, True),
            ((mp_count // 2, touch, emb), F32, True),
        ],
        [oht, ig, bag, cntta, cnttb],
    )

    group_size = dp_count * mp_count // 2
    rank_groups = [[g * 2 + c for g in range(group_size)] for c in range(2)]

    def exchange(x):
        return lax.all_to_all(
            x, both, split_axis=0, concat_axis=0, tiled=True, axis_index_groups=rank_groups
        )

    if near:
        rows_each = half_rows // group_size
        shape = (group_size, rows_each, emb)
        line = (dp_count // 2, rows_each, emb)
        pieces = call(
            split_near_kernel,
            [(line, F32, True)] * 4,
            [hot_keep.reshape(shape), hot_got.reshape(shape)],
        )
        pieces = [near_swap(x, k) if k else x for k, x in enumerate(pieces)]
        (part,) = call(sum_kernel, [(line, F32, True)], pieces)
        pieces = [far_swap(part, 2 * k) if k else part for k in range(4)]
        (part,) = call(sum_kernel, [(line, F32, True)], pieces)
        pieces = [near_swap(part, k) if k else part for k in range(4)]
        (half,) = call(order_near_kernel, [(shape, F32, True)], pieces)
        half = half.reshape(half_rows, emb)
    else:
        (chip,) = call(add_kernel, [((half_rows, emb), F32, True)], [hot_keep, hot_got])
        parts = exchange(chip.reshape(group_size, -1, emb))
        (shard,) = call(reduce_kernel, [(parts.shape, F32, True)], [parts])
        half = exchange(shard).reshape(half_rows, emb)
    other = swap(half, 1)
    hot_updated, hot_accum_new = call(
        final_kernel, [(hot_table.shape, F32, False)] * 2, [half, other, hot_table, hot_accum]
    )

    q_mat, slot_rows = call(
        lambda *r: bucket_kernel(slots, cap, *r),
        [((dp_count * cap, touch), BF16, True), ((dp_count * 8, emb), F32, True)],
        [pos],
    )
    touch_got = swap(touch_send, 1)
    mine, give = call(pair_kernel, [((touch, emb), F32, True)] * 2, [touch_keep, touch_got])
    got = swap(give, 2)
    (outgoing,) = call(
        lambda *r: pack_kernel(cap, *r),
        [((dp_count, cap + 8, emb), F32, True)],
        [mine, got, q_mat, slot_rows],
    )
    arrived = lax.all_to_all(outgoing, "dp", split_axis=0, concat_axis=0, tiled=True)
    cold_updated, cold_accum_new = call(
        lambda *r: cold_kernel(cap, *r),
        [(cold_table.shape, F32, False)] * 2,
        [arrived, cold_table, cold_accum],
    )
    return (hot_updated, hot_accum_new, cold_updated, cold_accum_new)


def solution(mesh):
    return whole(mesh)


def whole(mesh):
    return jax.shard_map(
        per_device,
        mesh=mesh,
        in_specs=(
            P("dp", None),
            P("dp", "mp", None),
            P("dp", "mp", None),
            P("dp", "mp", None),
            P(),
            P("dp", None),
            P(None, "mp"),
            P("mp"),
            P("mp", None),
            P(),
            P(),
            P(("dp", "mp"), None),
            P(("dp", "mp"), None),
        ),
        out_specs=(P(), P(), P(("dp", "mp"), None), P(("dp", "mp"), None)),
        check_vma=False,
    )
```

```python
import jax
import jax.numpy as jnp
from jax import lax
from jax.experimental import pallas as pl
from jax.experimental.pallas import tpu as pltpu
from jax.sharding import PartitionSpec as P

STEP_SIZE = 0.5
F32 = jnp.float32
BF16 = jnp.bfloat16
I32 = jnp.int32


def adagrad(table_rows, accum_rows, grad_rows):
    accum_new = accum_rows + grad_rows * grad_rows
    return (table_rows - STEP_SIZE * grad_rows / jnp.sqrt(accum_new), accum_new)


def loop(count, body, init):
    if count <= 16:
        for i in range(count):
            init = body(i, init)
        return init
    return lax.fori_loop(0, count, body, init)


def hi_lo(x):
    hi = x.astype(BF16)
    lo = (x - hi.astype(F32)).astype(BF16)
    return jnp.concatenate([hi, lo], axis=1)


def sum_halves(x):
    half = x.shape[1] // 2
    return x[:, :half] + x[:, half:]


def dot(a, b, dims=(((1,), (0,)), ((), ()))):
    return lax.dot_general(a, b, dims, preferred_element_type=F32)


NT = (((1,), (1,)), ((), ()))
TN = (((0,), (0,)), ((), ()))


def iota(shape, dim, dtype=I32):
    r = lax.broadcasted_iota(I32, shape, dim)
    return r if dtype == I32 else r.astype(dtype)


VM = pl.BlockSpec(memory_space=pltpu.VMEM)
ANY = pl.BlockSpec(memory_space=pl.ANY)


def call(body, outs, ins, scratch=(), late=(), raw=()):
    avals = [
        pltpu.VMEM(shape, dtype) if stay else jax.ShapeDtypeStruct(shape, dtype)
        for shape, dtype, stay in outs
    ]
    return pl.pallas_call(
        body,
        out_shape=avals,
        in_specs=[ANY if i in raw else VM for i in range(len(ins))],
        out_specs=[VM] * len(outs),
        scratch_shapes=scratch,
        compiler_params=pltpu.CompilerParams(vmem_limit_bytes=16 * 1024 * 1024),
    )(
        *[
            pltpu.with_memory_space_constraint(
                x, pltpu.HBM if i in late or i in raw else pltpu.VMEM
            )
            for i, x in enumerate(ins)
        ]
    )


def column(row):
    return jnp.broadcast_to(row, (8, row.shape[1])).T[:, 0:1]


def cast_kernel(count, *refs):
    sources, outs = refs[:count], refs[count : 2 * count]
    table_ref, sems = refs[2 * count :]
    copies = [
        pltpu.make_async_copy(src, outs[i] if i else table_ref, sems.at[i])
        for i, src in enumerate(sources)
    ]
    for copy in copies:
        copy.start()
    copies[0].wait()
    table = table_ref[...].astype(BF16)
    if len(outs[0].shape) == 2:
        outs[0][...] = table
    else:
        for o in range(outs[0].shape[0]):
            outs[0][o] = table
    for copy in copies[1:]:
        copy.wait()


def pack_rows(out_width, hidden, emb, item_rows):
    starts = [0, out_width // emb * hidden]
    starts.append(starts[-1] + -(-item_rows // 16) * 16)
    starts.append(starts[-1] + 16)
    return starts + [starts[-1] + 16]


def prep_kernel(at, v_ref, items_ref, sizes_ref, bias_ref, out_ref):
    hidden, width = v_ref.shape
    emb = out_ref.shape[1]
    for j in range(width // emb):
        out_ref[j * hidden : (j + 1) * hidden, :] = v_ref[:, j * emb : (j + 1) * emb]

    def padded(x, rows):
        if x.shape[0] == rows:
            return x
        return jnp.concatenate([x, jnp.zeros((rows - x.shape[0], emb), F32)], axis=0)

    items = items_ref[...].astype(F32)
    out_ref[at[1] : at[2], :] = padded(items, at[2] - at[1]).astype(BF16)
    out_ref[at[2] : at[3], :] = padded(sizes_ref[...].astype(F32), 16).astype(BF16)
    bias = bias_ref[...]
    hi = bias.astype(BF16).astype(F32)
    mid = (bias - hi).astype(BF16).astype(F32)
    low = bias - hi - mid
    out_ref[at[3] : at[4], :] = padded(jnp.concatenate([hi, mid, low], axis=0), 16).astype(BF16)


def place_kernel(
    mp_count, slots, share, map_ref, ids_ref, hot_hbm, hot_ids_hbm, weight_hbm, grads_hbm,
    pos_ref, row_ref, hot_ref, hot_ids_ref, weight_ref, grads_ref, sems,
):
    my = lax.axis_index("mp")
    mine = grads_hbm.at[pl.ds(pl.multiple_of(my * share, share), share), :]
    copies = [
        pltpu.make_async_copy(hot_hbm, hot_ref, sems.at[0]),
        pltpu.make_async_copy(hot_ids_hbm, hot_ids_ref, sems.at[1]),
        pltpu.make_async_copy(weight_hbm, weight_ref, sems.at[2]),
        pltpu.make_async_copy(mine, grads_ref, sems.at[3]),
    ]
    for copy in copies:
        copy.start()
    touch = ids_ref.shape[1]
    map_rows, lanes = map_ref.shape
    ids_col = column(ids_ref[...])
    in_row = (iota((touch, map_rows), 1) == ids_col // lanes).astype(F32)
    picked = lax.dot_general(
        in_row, map_ref[...].astype(F32), (((1,), (0,)), ((), ())),
        precision=lax.Precision.HIGHEST, preferred_element_type=F32,
    )
    in_lane = iota((touch, lanes), 1) == ids_col % lanes
    stored = jnp.sum(jnp.where(in_lane, picked, 0.0), axis=1, keepdims=True).astype(I32)
    stored = jnp.broadcast_to(stored, (touch, lanes))
    pos = stored // (mp_count * slots) * slots + stored % slots
    pos_ref[...] = pos
    row_ref[...] = pos.T[:8, :]
    for copy in copies:
        copy.wait()


def count_kernel(
    share, touch, at, item_rows, count_rows, p0, p1, cnt_ref, cntt_ref,
    items_ref, starts_ref, ends_ref, acc_ref,
):
    lanes = p0.shape[1]
    my = lax.axis_index("mp")
    per = share // lanes
    block = min(item_rows, -(-3 * item_rows // 8))
    sub_t = iota((touch, lanes), 0, F32)
    upto = (iota((lanes, lanes), 0) <= iota((lanes, lanes), 1)).astype(F32).astype(BF16)
    packs = (p0, p1)
    for k, pack in enumerate(packs):
        sizes = pack[at[2] : at[3], :]
        ends = dot(sizes, upto)[:count_rows]
        sizes = sizes.astype(F32)[:count_rows]
        totals = jnp.broadcast_to(jnp.sum(sizes, axis=1, keepdims=True), ends.shape)
        row = iota(ends.shape, 0)
        for r in range(count_rows - 1):
            ends = ends + jnp.where(row > r, totals[r : r + 1, :], 0.0)
        ends_ref[k] = ends
        starts_ref[k] = ends - sizes
        items_ref[k] = pack[at[1] : at[2], :].astype(F32)[:item_rows]

    def rows_of(ref, k):
        return jnp.concatenate([ref[k, pl.ds(my * per + j, 1), :] for j in range(per)], axis=1)

    bounds = []
    for k in range(len(packs)):
        starts = rows_of(starts_ref, k)
        ends = rows_of(ends_ref, k)
        first = jnp.min(starts).astype(I32) // lanes
        last = (jnp.max(ends).astype(I32) + lanes - 1) // lanes
        bounds.append((starts, ends, jnp.minimum(first, item_rows - block), last))

    def counted(k, first, rows, starts, ends):
        pick = jnp.concatenate(
            [
                (sub_t == items_ref[k, pl.ds(first + j, 1), :]).astype(F32).astype(BF16)
                for j in range(rows)
            ],
            axis=1,
        )
        pos = iota((rows * lanes, share), 0, F32) + (first * lanes).astype(F32)
        memb = ((pos >= starts) & (pos < ends)).astype(F32).astype(BF16)
        return dot(pick, memb)

    for k, (starts, ends, first, last) in enumerate(bounds):
        acc_ref[...] = counted(k, first, block, starts, ends)

        def body(c, carry):
            acc_ref[...] += counted(k, c, 1, starts, ends)
            return carry

        lax.fori_loop(first + block, last, body, 0)
        counts_t = acc_ref[...]
        cntt_ref[k * touch : (k + 1) * touch, :] = counts_t.astype(BF16)
        cnt_ref[:, k * touch : (k + 1) * touch] = counts_t.T.astype(BF16)


def pre_kernel(
    share, at, hidden, w0, w1, w2, w3, p0, p1, p2, p3, grads_ref, rows_ref,
    wt_ref, tail_ref, pre_ref, back_ref,
):
    emb = p0.shape[1]
    hot_cols = rows_ref.shape[0]
    grads = grads_ref[...]
    rows = rows_ref[...]
    for k, (w, p) in enumerate(zip((w0, w1, w2, w3), (p0, p1, p2, p3))):
        cols = slice(k * hidden, (k + 1) * hidden)
        bias = jnp.sum(p[at[3] : at[4], :].astype(F32), axis=0, keepdims=True)
        pre_ref[:, cols] = dot(rows, w[:hot_cols, :], TN) + bias
        back = jnp.zeros((share, hidden), F32)
        for j in range(grads.shape[1] // emb):
            piece = p[j * hidden : (j + 1) * hidden, :]
            back = back + dot(grads[:, j * emb : (j + 1) * emb], piece, NT)
        back_ref[:, cols] = back
        tail_ref[:, cols] = w[hot_cols:, :]
        wt_ref[cols, :] = w[...].astype(F32).T.astype(BF16)


def fetch_kernel(pos_ref, table_ref, out_ref):
    owners, slots, _ = table_ref.shape

    def body(o, acc):
        return acc + dot(hits(pos_ref[...], o * slots, slots), table_ref[o])

    out_ref[...] = loop(owners, body, jnp.zeros(out_ref.shape, F32)).astype(BF16)


def fetch_near_kernel(pos_ref, row_ref, *refs):
    tables, (mine_ref, give_ref) = refs[:-2], refs[-2:]
    touch, lanes = pos_ref.shape
    slots = tables[0].shape[0]
    my = lax.axis_index("dp")
    theirs = jnp.broadcast_to(row_ref[...].T[:, 0:1], (touch, lanes))
    both = jnp.concatenate([pos_ref[...], theirs], axis=0)
    acc = jnp.zeros((2 * touch, mine_ref.shape[1]), F32)
    for k, table in enumerate(tables):
        acc = acc + dot(hits(both, (my ^ (2 * k)) * slots, slots), table[...])
    mine_ref[...] = acc[:touch].astype(BF16)
    give_ref[...] = acc[touch:].astype(BF16)


def join_kernel(mine_ref, near_ref, far_ref, cross_ref, out_ref):
    out_ref[0] = (mine_ref[...].astype(F32) + near_ref[...].astype(F32)).astype(BF16)
    out_ref[1] = (far_ref[...].astype(F32) + cross_ref[...].astype(F32)).astype(BF16)


def hits(pos, first, slots):
    rel = pos - first
    lane = iota(rel.shape, 1)
    lanes = rel.shape[1]
    return jnp.concatenate(
        [(lane + j * lanes == rel).astype(F32).astype(BF16) for j in range(slots // lanes)], axis=1
    )


def onehot_kernel(share, fields, ids_ref, hot_ref, out_ref, rows_ref):
    my = lax.axis_index("mp")
    emb = hot_ref.shape[1]
    hot = hot_ref[...].T.astype(BF16)
    sub = iota((out_ref.shape[0], share), 0)
    for f in range(fields):
        mine = ids_ref[f : f + 1, pl.ds(pl.multiple_of(my * share, share), share)]
        hit = (sub == mine).astype(F32).astype(BF16)
        out_ref[:, f * share : (f + 1) * share] = hit
        rows_ref[f * emb : (f + 1) * emb, :] = dot(hot, hit).astype(BF16)


def bucket_kernel(slots, cap, pos_ref, q_ref, srow_ref):
    pos = pos_ref[...]
    touch, lanes = pos.shape
    row = pos.T[0:1, :]
    owner = row // slots
    before = iota((touch, touch), 0) < iota((touch, touch), 1)
    rank = jnp.sum(
        ((pos[:, 0:1] // slots == owner) & before).astype(F32), axis=0, keepdims=True
    )
    bucket = owner.astype(F32) * float(cap) + rank
    q_ref[...] = (iota(q_ref.shape, 0, F32) == bucket).astype(F32).astype(BF16)
    at_rank = (iota((touch, lanes), 1, F32) == column(rank)).astype(F32)
    mine = jnp.where(
        iota((srow_ref.shape[0], touch), 0) // 8 == owner, (row % slots).astype(F32), 0.0
    )
    srow_ref[...] = lax.dot_general(
        mine, at_rank, (((1,), (0,)), ((), ())),
        precision=lax.Precision.HIGHEST, preferred_element_type=F32,
    )


def main_kernel(
    fields, cnta_ref, cntb_ref, mine_ref, core_ref, pre_ref, back_ref, tail_ref, wt_ref, oht_ref,
    ig_ref, bag_ref, send_ref,
):
    _, touch, emb = mine_ref.shape
    share = cnta_ref.shape[0]
    core = lax.axis_index("mp") % 2
    pooled = jnp.zeros((share, emb), F32)
    for k in range(4):
        cnt = (cnta_ref, cntb_ref)[k // 2]
        rows = (mine_ref, core_ref)[k % 2][k // 2]
        pooled = pooled + dot(cnt[:, k % 2 * touch : (k % 2 + 1) * touch], rows)
    pre = pre_ref[...] + dot(pooled.astype(BF16), tail_ref[...])
    sig = jax.nn.sigmoid(pre)
    hidden = (back_ref[...] * sig * (1.0 + pre * (1.0 - sig))).astype(BF16)
    grad = dot(hidden, wt_ref[...])
    for f in range(fields):
        ig_ref[f * share : (f + 1) * share, :] = hi_lo(grad[:, f * emb : (f + 1) * emb])
    bag_ref[...] = hi_lo(grad[:, fields * emb :])
    half = send_ref.shape[0]
    first = pl.multiple_of((1 - core) * half, half)
    send_ref[...] = sum_halves(dot(oht_ref[pl.ds(first, half), :], ig_ref[...]))


def keep_kernel(oht_ref, ig_ref, bag_ref, cntta_ref, cnttb_ref, keep_ref, touch_send, touch_keep):
    half = keep_ref.shape[0]
    core = lax.axis_index("mp") % 2
    first = pl.multiple_of(core * half, half)
    keep_ref[...] = sum_halves(dot(oht_ref[pl.ds(first, half), :], ig_ref[...]))
    touch = touch_send.shape[1]
    for k in range(4):
        ref = touch_send if k % 2 else touch_keep
        counts = (cntta_ref, cnttb_ref)[k // 2]
        rows = slice(k % 2 * touch, (k % 2 + 1) * touch)
        ref[k // 2] = sum_halves(dot(counts[rows, :], bag_ref[...]))


def add_kernel(a_ref, b_ref, out_ref):
    out_ref[...] = a_ref[...] + b_ref[...]


def pair_kernel(keep_ref, got_ref, mine_ref, give_ref):
    mine_ref[...] = keep_ref[0] + got_ref[0]
    give_ref[...] = keep_ref[1] + got_ref[1]


def fetch_kernel(pos_ref, table_ref, out_ref):
    owners, slots, emb = table_ref.shape
    touch, lanes = pos_ref.shape
    lane = iota((touch, lanes), 1)

    def body(o, acc):
        rel = pos_ref[...] - o * slots
        hit = jnp.concatenate(
            [
                (lane + j * lanes == rel).astype(F32).astype(BF16)
                for j in range(slots // lanes)
            ],
            axis=1,
        )
        return acc + dot(hit, table_ref[o])

    out_ref[...] = loop(owners, body, jnp.zeros((touch, emb), F32)).astype(BF16)


def reduce_kernel(parts_ref, out_ref):
    total = jnp.sum(parts_ref[...], axis=0, keepdims=True)
    out_ref[...] = jnp.broadcast_to(total, out_ref.shape)


def near_place(far, k):
    near = lax.axis_index("dp") % 2
    group = lax.axis_index("mp") // 2
    return (far * 2 + (near ^ (k // 2))) * 2 + (group ^ (k % 2))


def split_near_kernel(keep_ref, got_ref, *outs):
    for k, ref in enumerate(outs):
        for far in range(ref.shape[0]):
            at = near_place(far, k)
            ref[far] = keep_ref[at] + got_ref[at]


def sum_kernel(a_ref, b_ref, c_ref, d_ref, out_ref):
    out_ref[...] = (a_ref[...] + b_ref[...]) + (c_ref[...] + d_ref[...])


def order_near_kernel(*refs):
    for k, ref in enumerate(refs[:-1]):
        for far in range(ref.shape[0]):
            refs[-1][near_place(far, k)] = ref[far]


def pack_kernel(cap, mine_ref, got_ref, q_ref, srow_ref, out_ref):
    owners = out_ref.shape[0]
    emb = out_ref.shape[2]
    rows = sum_halves(dot(q_ref[...], hi_lo(mine_ref[...] + got_ref[...])))
    out_ref[:, :cap, :] = rows.reshape(owners, cap, emb)
    out_ref[:, cap:, :] = srow_ref[...].reshape(owners, 8, emb)


def cold_kernel(cap, arrived_ref, table_ref, accum_ref, new_ref, acc_ref):
    slots, emb = table_ref.shape
    sub = iota((slots, cap), 0, F32)

    def body(d, acc):
        slot = arrived_ref[d, cap : cap + 1, :][:, :cap]
        hit = (sub == slot).astype(F32).astype(BF16)
        return acc + dot(hit, hi_lo(arrived_ref[d, :cap, :]))

    grad = sum_halves(loop(arrived_ref.shape[0], body, jnp.zeros((slots, 2 * emb), F32)))
    new_ref[...], acc_ref[...] = adagrad(table_ref[...], accum_ref[...], grad)


def final_kernel(mine_ref, theirs_ref, table_ref, accum_ref, new_ref, acc_ref):
    half = mine_ref.shape[0]
    core = lax.axis_index("mp") % 2
    for ref, c in ((mine_ref, core), (theirs_ref, 1 - core)):
        at = pl.ds(pl.multiple_of(c * half, half), half)
        new_ref[at, :], acc_ref[at, :] = adagrad(table_ref[at, :], accum_ref[at, :], ref[...])


def per_device(
    hot_ids,
    touched,
    cold_items,
    bag_counts,
    owner_map,
    grad_out,
    weight_in,
    bias_in,
    weight_out,
    hot_table,
    hot_accum,
    cold_table,
    cold_accum,
):
    dp_count = lax.axis_size("dp")
    mp_count = lax.axis_size("mp")
    slots, emb = cold_table.shape
    samples, fields = hot_ids.shape
    touch = touched.shape[2]
    items = cold_items.shape[2]
    d_in, hidden = weight_in.shape
    all_hidden = mp_count * hidden
    hot_rows = hot_table.shape[0]
    share = samples // mp_count
    cap = -(-(2 * touch // dp_count) // 8) * 8
    item_rows = items // emb
    count_rows = samples // emb
    both = ("dp", "mp")

    def swap(x, mask):
        return lax.ppermute(x, "mp", [(i, i ^ mask) for i in range(mp_count)])

    def far_swap(x, mask):
        return lax.ppermute(x, "dp", [(i, i ^ mask) for i in range(dp_count)])

    def near_swap(x, k):
        mask = k // 2 * mp_count + k % 2 * 2
        return lax.ppermute(x, both, [(i, i ^ mask) for i in range(dp_count * mp_count)])

    near = dp_count == 8 and mp_count == 4

    small = [
        owner_map.reshape(-1, emb),
        touched.reshape(1, touch),
        weight_out,
        cold_items.reshape(item_rows, emb),
        bag_counts.reshape(count_rows, emb),
        bias_in.reshape(1, hidden),
    ]
    own, *small = call(
        lambda *r: cast_kernel(1 + len(small), *r),
        [((slots, emb) if near else (dp_count, slots, emb), BF16, near)]
        + [(x.shape, x.dtype, True) for x in small],
        [cold_table, *small],
        raw=range(1 + len(small)),
        scratch=[
            pltpu.VMEM((slots, emb), F32),
            pltpu.SemaphoreType.DMA((1 + len(small),)),
        ],
    )
    map_rows, touched_row, *small = small
    if near:
        tables = [own]
        for k in (2, 4, 6):
            tables.append(far_swap(own, k))
    else:
        tables = lax.all_to_all(own, "dp", split_axis=0, concat_axis=0, tiled=True)

    w_far = swap(weight_in, 2)
    w_near = swap(weight_in, 1)
    weights = [weight_in, w_near, w_far, swap(w_far, 1)]
    at = pack_rows(weight_out.shape[1], hidden, emb, item_rows)
    (pack,) = call(lambda *r: prep_kernel(at, *r), [((at[-1], emb), BF16, True)], small)
    pack_far = swap(pack, 2)
    pack_near = swap(pack, 1)
    packs = [pack, pack_near, pack_far, swap(pack_far, 1)]

    pos, pos_row, hot_near, ids_near, weight_near, grads_near = call(
        lambda *r: place_kernel(mp_count, slots, share, *r),
        [
            ((touch, emb), I32, True),
            ((8, touch), I32, True),
            (hot_table.shape, F32, True),
            ((fields, samples), I32, True),
            (weight_in.shape, BF16, True),
            ((share, grad_out.shape[1]), BF16, True),
        ],
        [map_rows, touched_row, hot_table, hot_ids.T, weight_in, grad_out],
        raw=range(2, 6),
        scratch=[pltpu.SemaphoreType.DMA((4,))],
    )
    weights[0] = weight_near

    def count(pair):
        return call(
            lambda *r: count_kernel(share, touch, at, item_rows, count_rows, *r),
            [((share, 2 * touch), BF16, True), ((2 * touch, share), BF16, True)],
            pair,
            scratch=[
                pltpu.VMEM((2, item_rows, emb), F32),
                pltpu.VMEM((2, count_rows, emb), F32),
                pltpu.VMEM((2, count_rows, emb), F32),
                pltpu.VMEM((touch, share), F32),
            ],
        )

    cnta, cntta = count(packs[:2])
    cntb, cnttb = count(packs[2:])

    oht, rows = call(
        lambda *r: onehot_kernel(share, fields, *r),
        [((hot_rows, fields * share), BF16, True), ((fields * emb, share), BF16, True)],
        [ids_near, hot_near],
    )

    wt, tail, pre, back = call(
        lambda *r: pre_kernel(share, at, hidden, *r),
        [
            ((all_hidden, d_in), BF16, True),
            ((emb, all_hidden), BF16, True),
            ((share, all_hidden), F32, True),
            ((share, all_hidden), F32, True),
        ],
        [*weights, *packs, grads_near, rows],
    )

    if near:
        other_row = far_swap(pos_row, 1)
        mine, give = call(
            fetch_near_kernel, [((touch, emb), BF16, True)] * 2, [pos, other_row, *tables]
        )
        from_near = near_swap(give, 2)
        from_far = near_swap(mine, 1)
        from_cross = near_swap(give, 3)
        (fetched,) = call(
            join_kernel, [((2, touch, emb), BF16, True)], [mine, from_near, from_far, from_cross]
        )
    else:
        (mine,) = call(fetch_kernel, [((touch, emb), BF16, True)], [pos, tables], late=(1,))
        fetched = jnp.stack([mine, swap(mine, 2)])
    fetched_core = swap(fetched, 1)

    half_rows = hot_rows // 2
    ig, bag, hot_send = call(
        lambda *r: main_kernel(fields, *r),
        [
            ((fields * share, 2 * emb), BF16, True),
            ((share, 2 * emb), BF16, True),
            ((half_rows, emb), F32, True),
        ],
        [cnta, cntb, fetched, fetched_core, pre, back, tail, wt, oht],
    )
    hot_got = swap(hot_send, 1)
    hot_keep, touch_send, touch_keep = call(
        keep_kernel,
        [
            ((half_rows, emb), F32, True),
            ((mp_count // 2, touch, emb), F32, True),
            ((mp_count // 2, touch, emb), F32, True),
        ],
        [oht, ig, bag, cntta, cnttb],
    )

    group_size = dp_count * mp_count // 2
    rank_groups = [[g * 2 + c for g in range(group_size)] for c in range(2)]

    def exchange(x):
        return lax.all_to_all(
            x, both, split_axis=0, concat_axis=0, tiled=True, axis_index_groups=rank_groups
        )

    if near:
        rows_each = half_rows // group_size
        shape = (group_size, rows_each, emb)
        line = (dp_count // 2, rows_each, emb)
        pieces = call(
            split_near_kernel,
            [(line, F32, True)] * 4,
            [hot_keep.reshape(shape), hot_got.reshape(shape)],
        )
        pieces = [near_swap(x, k) if k else x for k, x in enumerate(pieces)]
        (part,) = call(sum_kernel, [(line, F32, True)], pieces)
        pieces = [part]
        for k in (1, 2, 3):
            pieces.append(far_swap(part, 2 * k))
        (part,) = call(sum_kernel, [(line, F32, True)], pieces)
        pieces = [near_swap(part, k) if k else part for k in range(4)]
        (half,) = call(order_near_kernel, [(shape, F32, True)], pieces)
        half = half.reshape(half_rows, emb)
    else:
        (chip,) = call(add_kernel, [((half_rows, emb), F32, True)], [hot_keep, hot_got])
        parts = exchange(chip.reshape(group_size, -1, emb))
        (shard,) = call(reduce_kernel, [(parts.shape, F32, True)], [parts])
        half = exchange(shard).reshape(half_rows, emb)
    other = swap(half, 1)
    hot_updated, hot_accum_new = call(
        final_kernel, [(hot_table.shape, F32, False)] * 2, [half, other, hot_table, hot_accum]
    )

    q_mat, slot_rows = call(
        lambda *r: bucket_kernel(slots, cap, *r),
        [((dp_count * cap, touch), BF16, True), ((dp_count * 8, emb), F32, True)],
        [pos],
    )
    touch_got = swap(touch_send, 1)
    mine, give = call(pair_kernel, [((touch, emb), F32, True)] * 2, [touch_keep, touch_got])
    got = swap(give, 2)
    (outgoing,) = call(
        lambda *r: pack_kernel(cap, *r),
        [((dp_count, cap + 8, emb), F32, True)],
        [mine, got, q_mat, slot_rows],
    )
    arrived = lax.all_to_all(outgoing, "dp", split_axis=0, concat_axis=0, tiled=True)
    cold_updated, cold_accum_new = call(
        lambda *r: cold_kernel(cap, *r),
        [(cold_table.shape, F32, False)] * 2,
        [arrived, cold_table, cold_accum],
    )
    return (hot_updated, hot_accum_new, cold_updated, cold_accum_new)


def solution(mesh):
    return whole(mesh)


def whole(mesh):
    return jax.shard_map(
        per_device,
        mesh=mesh,
        in_specs=(
            P("dp", None),
            P("dp", "mp", None),
            P("dp", "mp", None),
            P("dp", "mp", None),
            P(),
            P("dp", None),
            P(None, "mp"),
            P("mp"),
            P("mp", None),
            P(),
            P(),
            P(("dp", "mp"), None),
            P(("dp", "mp"), None),
        ),
        out_specs=(P(), P(), P(("dp", "mp"), None), P(("dp", "mp"), None)),
        check_vma=False,
    )
```

```python
import jax
import jax.numpy as jnp
from jax import lax
from jax.experimental import pallas as pl
from jax.experimental.pallas import tpu as pltpu
from jax.sharding import PartitionSpec as P

STEP_SIZE = 0.5
F32 = jnp.float32
BF16 = jnp.bfloat16
I32 = jnp.int32


def adagrad(table_rows, accum_rows, grad_rows):
    accum_new = accum_rows + grad_rows * grad_rows
    return (table_rows - STEP_SIZE * grad_rows / jnp.sqrt(accum_new), accum_new)


def loop(count, body, init):
    if count <= 16:
        for i in range(count):
            init = body(i, init)
        return init
    return lax.fori_loop(0, count, body, init)


def hi_lo(x):
    hi = x.astype(BF16)
    lo = (x - hi.astype(F32)).astype(BF16)
    return jnp.concatenate([hi, lo], axis=1)


def sum_halves(x):
    half = x.shape[1] // 2
    return x[:, :half] + x[:, half:]


def dot(a, b, dims=(((1,), (0,)), ((), ()))):
    return lax.dot_general(a, b, dims, preferred_element_type=F32)


NT = (((1,), (1,)), ((), ()))
TN = (((0,), (0,)), ((), ()))


def iota(shape, dim, dtype=I32):
    r = lax.broadcasted_iota(I32, shape, dim)
    return r if dtype == I32 else r.astype(dtype)


VM = pl.BlockSpec(memory_space=pltpu.VMEM)
ANY = pl.BlockSpec(memory_space=pl.ANY)


def call(body, outs, ins, scratch=(), late=(), raw=()):
    avals = [
        pltpu.VMEM(shape, dtype) if stay else jax.ShapeDtypeStruct(shape, dtype)
        for shape, dtype, stay in outs
    ]
    return pl.pallas_call(
        body,
        out_shape=avals,
        in_specs=[ANY if i in raw else VM for i in range(len(ins))],
        out_specs=[VM] * len(outs),
        scratch_shapes=scratch,
        compiler_params=pltpu.CompilerParams(vmem_limit_bytes=16 * 1024 * 1024),
    )(
        *[
            pltpu.with_memory_space_constraint(
                x, pltpu.HBM if i in late or i in raw else pltpu.VMEM
            )
            for i, x in enumerate(ins)
        ]
    )


def column(row):
    return jnp.broadcast_to(row, (8, row.shape[1])).T[:, 0:1]


def cast_kernel(count, *refs):
    sources, outs = refs[:count], refs[count : 2 * count]
    table_ref, sems = refs[2 * count :]
    copies = [
        pltpu.make_async_copy(src, outs[i] if i else table_ref, sems.at[i])
        for i, src in enumerate(sources)
    ]
    for copy in copies:
        copy.start()
    copies[0].wait()
    table = table_ref[...].astype(BF16)
    if len(outs[0].shape) == 2:
        outs[0][...] = table
    else:
        for o in range(outs[0].shape[0]):
            outs[0][o] = table
    for copy in copies[1:]:
        copy.wait()


def pack_rows(out_width, hidden, emb, item_rows):
    starts = [0, out_width // emb * hidden]
    starts.append(starts[-1] + -(-item_rows // 16) * 16)
    starts.append(starts[-1] + 16)
    return starts + [starts[-1] + 16]


def prep_kernel(at, v_ref, items_ref, sizes_ref, bias_ref, out_ref):
    hidden, width = v_ref.shape
    emb = out_ref.shape[1]
    for j in range(width // emb):
        out_ref[j * hidden : (j + 1) * hidden, :] = v_ref[:, j * emb : (j + 1) * emb]

    def padded(x, rows):
        if x.shape[0] == rows:
            return x
        return jnp.concatenate([x, jnp.zeros((rows - x.shape[0], emb), F32)], axis=0)

    items = items_ref[...].astype(F32)
    out_ref[at[1] : at[2], :] = padded(items, at[2] - at[1]).astype(BF16)
    out_ref[at[2] : at[3], :] = padded(sizes_ref[...].astype(F32), 16).astype(BF16)
    bias = bias_ref[...]
    hi = bias.astype(BF16).astype(F32)
    mid = (bias - hi).astype(BF16).astype(F32)
    low = bias - hi - mid
    out_ref[at[3] : at[4], :] = padded(jnp.concatenate([hi, mid, low], axis=0), 16).astype(BF16)


def place_kernel(mp_count, slots, map_ref, ids_ref, pos_ref, row_ref):
    touch = ids_ref.shape[1]
    map_rows, lanes = map_ref.shape
    ids_col = column(ids_ref[...])
    in_row = (iota((touch, map_rows), 1) == ids_col // lanes).astype(F32)
    picked = lax.dot_general(
        in_row, map_ref[...].astype(F32), (((1,), (0,)), ((), ())),
        precision=lax.Precision.HIGHEST, preferred_element_type=F32,
    )
    in_lane = iota((touch, lanes), 1) == ids_col % lanes
    stored = jnp.sum(jnp.where(in_lane, picked, 0.0), axis=1, keepdims=True).astype(I32)
    stored = jnp.broadcast_to(stored, (touch, lanes))
    pos = stored // (mp_count * slots) * slots + stored % slots
    pos_ref[...] = pos
    row_ref[...] = pos.T[:8, :]


def load_kernel(
    share, hot_hbm, hot_ids_hbm, weight_hbm, grads_hbm,
    hot_ref, hot_ids_ref, weight_ref, grads_ref, sems,
):
    my = lax.axis_index("mp")
    mine = grads_hbm.at[pl.ds(pl.multiple_of(my * share, share), share), :]
    copies = [
        pltpu.make_async_copy(hot_hbm, hot_ref, sems.at[0]),
        pltpu.make_async_copy(hot_ids_hbm, hot_ids_ref, sems.at[1]),
        pltpu.make_async_copy(weight_hbm, weight_ref, sems.at[2]),
        pltpu.make_async_copy(mine, grads_ref, sems.at[3]),
    ]
    for copy in copies:
        copy.start()
    for copy in copies:
        copy.wait()


def count_kernel(
    share, touch, at, item_rows, count_rows, p0, p1, cnt_ref, cntt_ref,
    items_ref, starts_ref, ends_ref, acc_ref,
):
    lanes = p0.shape[1]
    my = lax.axis_index("mp")
    per = share // lanes
    block = min(item_rows, -(-3 * item_rows // 8))
    sub_t = iota((touch, lanes), 0, F32)
    upto = (iota((lanes, lanes), 0) <= iota((lanes, lanes), 1)).astype(F32).astype(BF16)
    packs = (p0, p1)
    for k, pack in enumerate(packs):
        sizes = pack[at[2] : at[3], :]
        ends = dot(sizes, upto)[:count_rows]
        sizes = sizes.astype(F32)[:count_rows]
        totals = jnp.broadcast_to(jnp.sum(sizes, axis=1, keepdims=True), ends.shape)
        row = iota(ends.shape, 0)
        for r in range(count_rows - 1):
            ends = ends + jnp.where(row > r, totals[r : r + 1, :], 0.0)
        ends_ref[k] = ends
        starts_ref[k] = ends - sizes
        items_ref[k] = pack[at[1] : at[2], :].astype(F32)[:item_rows]

    def rows_of(ref, k):
        return jnp.concatenate([ref[k, pl.ds(my * per + j, 1), :] for j in range(per)], axis=1)

    bounds = []
    for k in range(len(packs)):
        starts = rows_of(starts_ref, k)
        ends = rows_of(ends_ref, k)
        first = jnp.min(starts).astype(I32) // lanes
        last = (jnp.max(ends).astype(I32) + lanes - 1) // lanes
        bounds.append((starts, ends, jnp.minimum(first, item_rows - block), last))

    def counted(k, first, rows, starts, ends):
        pick = jnp.concatenate(
            [
                (sub_t == items_ref[k, pl.ds(first + j, 1), :]).astype(F32).astype(BF16)
                for j in range(rows)
            ],
            axis=1,
        )
        pos = iota((rows * lanes, share), 0, F32) + (first * lanes).astype(F32)
        memb = ((pos >= starts) & (pos < ends)).astype(F32).astype(BF16)
        return dot(pick, memb)

    for k, (starts, ends, first, last) in enumerate(bounds):
        acc_ref[...] = counted(k, first, block, starts, ends)

        def body(c, carry):
            acc_ref[...] += counted(k, c, 1, starts, ends)
            return carry

        lax.fori_loop(first + block, last, body, 0)
        counts_t = acc_ref[...]
        cntt_ref[k * touch : (k + 1) * touch, :] = counts_t.astype(BF16)
        cnt_ref[:, k * touch : (k + 1) * touch] = counts_t.T.astype(BF16)


def pre_kernel(
    share, at, hidden, w0, w1, w2, w3, p0, p1, p2, p3, grads_ref, rows_ref,
    wt_ref, tail_ref, pre_ref, back_ref,
):
    emb = p0.shape[1]
    hot_cols = rows_ref.shape[0]
    grads = grads_ref[...]
    rows = rows_ref[...]
    for k, (w, p) in enumerate(zip((w0, w1, w2, w3), (p0, p1, p2, p3))):
        cols = slice(k * hidden, (k + 1) * hidden)
        bias = jnp.sum(p[at[3] : at[4], :].astype(F32), axis=0, keepdims=True)
        pre_ref[:, cols] = dot(rows, w[:hot_cols, :], TN) + bias
        back = jnp.zeros((share, hidden), F32)
        for j in range(grads.shape[1] // emb):
            piece = p[j * hidden : (j + 1) * hidden, :]
            back = back + dot(grads[:, j * emb : (j + 1) * emb], piece, NT)
        back_ref[:, cols] = back
        tail_ref[:, cols] = w[hot_cols:, :]
        wt_ref[cols, :] = w[...].astype(F32).T.astype(BF16)


def fetch_kernel(pos_ref, table_ref, out_ref):
    owners, slots, _ = table_ref.shape

    def body(o, acc):
        return acc + dot(hits(pos_ref[...], o * slots, slots), table_ref[o])

    out_ref[...] = loop(owners, body, jnp.zeros(out_ref.shape, F32)).astype(BF16)


def fetch_near_kernel(pos_ref, row_ref, *refs):
    tables, (mine_ref, give_ref) = refs[:-2], refs[-2:]
    touch, lanes = pos_ref.shape
    slots = tables[0].shape[0]
    my = lax.axis_index("dp")
    theirs = jnp.broadcast_to(row_ref[...].T[:, 0:1], (touch, lanes))
    both = jnp.concatenate([pos_ref[...], theirs], axis=0)
    acc = jnp.zeros((2 * touch, mine_ref.shape[1]), F32)
    for k, table in enumerate(tables):
        acc = acc + dot(hits(both, (my ^ (2 * k)) * slots, slots), table[...])
    mine_ref[...] = acc[:touch].astype(BF16)
    give_ref[...] = acc[touch:].astype(BF16)


def join_kernel(mine_ref, near_ref, far_ref, cross_ref, out_ref):
    out_ref[0] = (mine_ref[...].astype(F32) + near_ref[...].astype(F32)).astype(BF16)
    out_ref[1] = (far_ref[...].astype(F32) + cross_ref[...].astype(F32)).astype(BF16)


def hits(pos, first, slots):
    rel = pos - first
    lane = iota(rel.shape, 1)
    lanes = rel.shape[1]
    return jnp.concatenate(
        [(lane + j * lanes == rel).astype(F32).astype(BF16) for j in range(slots // lanes)], axis=1
    )


def onehot_kernel(share, fields, ids_ref, hot_ref, out_ref, rows_ref):
    my = lax.axis_index("mp")
    emb = hot_ref.shape[1]
    hot = hot_ref[...].T.astype(BF16)
    sub = iota((out_ref.shape[0], share), 0)
    for f in range(fields):
        mine = ids_ref[f : f + 1, pl.ds(pl.multiple_of(my * share, share), share)]
        hit = (sub == mine).astype(F32).astype(BF16)
        out_ref[:, f * share : (f + 1) * share] = hit
        rows_ref[f * emb : (f + 1) * emb, :] = dot(hot, hit).astype(BF16)


def bucket_kernel(slots, cap, pos_ref, q_ref, srow_ref):
    pos = pos_ref[...]
    touch, lanes = pos.shape
    row = pos.T[0:1, :]
    owner = row // slots
    before = iota((touch, touch), 0) < iota((touch, touch), 1)
    rank = jnp.sum(
        ((pos[:, 0:1] // slots == owner) & before).astype(F32), axis=0, keepdims=True
    )
    bucket = owner.astype(F32) * float(cap) + rank
    q_ref[...] = (iota(q_ref.shape, 0, F32) == bucket).astype(F32).astype(BF16)
    at_rank = (iota((touch, lanes), 1, F32) == column(rank)).astype(F32)
    mine = jnp.where(
        iota((srow_ref.shape[0], touch), 0) // 8 == owner, (row % slots).astype(F32), 0.0
    )
    srow_ref[...] = lax.dot_general(
        mine, at_rank, (((1,), (0,)), ((), ())),
        precision=lax.Precision.HIGHEST, preferred_element_type=F32,
    )


def main_kernel(
    fields, cnta_ref, cntb_ref, mine_ref, core_ref, pre_ref, back_ref, tail_ref, wt_ref, oht_ref,
    ig_ref, bag_ref, send_ref,
):
    _, touch, emb = mine_ref.shape
    share = cnta_ref.shape[0]
    core = lax.axis_index("mp") % 2
    pooled = jnp.zeros((share, emb), F32)
    for k in range(4):
        cnt = (cnta_ref, cntb_ref)[k // 2]
        rows = (mine_ref, core_ref)[k % 2][k // 2]
        pooled = pooled + dot(cnt[:, k % 2 * touch : (k % 2 + 1) * touch], rows)
    pre = pre_ref[...] + dot(pooled.astype(BF16), tail_ref[...])
    sig = jax.nn.sigmoid(pre)
    hidden = (back_ref[...] * sig * (1.0 + pre * (1.0 - sig))).astype(BF16)
    grad = dot(hidden, wt_ref[...])
    for f in range(fields):
        ig_ref[f * share : (f + 1) * share, :] = hi_lo(grad[:, f * emb : (f + 1) * emb])
    bag_ref[...] = hi_lo(grad[:, fields * emb :])
    half = send_ref.shape[0]
    first = pl.multiple_of((1 - core) * half, half)
    send_ref[...] = sum_halves(dot(oht_ref[pl.ds(first, half), :], ig_ref[...]))


def keep_kernel(oht_ref, ig_ref, bag_ref, cntta_ref, cnttb_ref, keep_ref, touch_send, touch_keep):
    half = keep_ref.shape[0]
    core = lax.axis_index("mp") % 2
    first = pl.multiple_of(core * half, half)
    keep_ref[...] = sum_halves(dot(oht_ref[pl.ds(first, half), :], ig_ref[...]))
    touch = touch_send.shape[1]
    for k in range(4):
        ref = touch_send if k % 2 else touch_keep
        counts = (cntta_ref, cnttb_ref)[k // 2]
        rows = slice(k % 2 * touch, (k % 2 + 1) * touch)
        ref[k // 2] = sum_halves(dot(counts[rows, :], bag_ref[...]))


def add_kernel(a_ref, b_ref, out_ref):
    out_ref[...] = a_ref[...] + b_ref[...]


def pair_kernel(keep_ref, got_ref, mine_ref, give_ref):
    mine_ref[...] = keep_ref[0] + got_ref[0]
    give_ref[...] = keep_ref[1] + got_ref[1]


def fetch_kernel(pos_ref, table_ref, out_ref):
    owners, slots, emb = table_ref.shape
    touch, lanes = pos_ref.shape
    lane = iota((touch, lanes), 1)

    def body(o, acc):
        rel = pos_ref[...] - o * slots
        hit = jnp.concatenate(
            [
                (lane + j * lanes == rel).astype(F32).astype(BF16)
                for j in range(slots // lanes)
            ],
            axis=1,
        )
        return acc + dot(hit, table_ref[o])

    out_ref[...] = loop(owners, body, jnp.zeros((touch, emb), F32)).astype(BF16)


def reduce_kernel(parts_ref, out_ref):
    total = jnp.sum(parts_ref[...], axis=0, keepdims=True)
    out_ref[...] = jnp.broadcast_to(total, out_ref.shape)


def near_place(far, k):
    near = lax.axis_index("dp") % 2
    group = lax.axis_index("mp") // 2
    return (far * 2 + (near ^ (k // 2))) * 2 + (group ^ (k % 2))


def split_near_kernel(keep_ref, got_ref, *outs):
    for k, ref in enumerate(outs):
        for far in range(ref.shape[0]):
            at = near_place(far, k)
            ref[far] = keep_ref[at] + got_ref[at]


def sum_kernel(a_ref, b_ref, c_ref, d_ref, out_ref):
    out_ref[...] = (a_ref[...] + b_ref[...]) + (c_ref[...] + d_ref[...])


def order_near_kernel(*refs):
    for k, ref in enumerate(refs[:-1]):
        for far in range(ref.shape[0]):
            refs[-1][near_place(far, k)] = ref[far]


def pack_kernel(cap, mine_ref, got_ref, q_ref, srow_ref, out_ref):
    owners = out_ref.shape[0]
    emb = out_ref.shape[2]
    rows = sum_halves(dot(q_ref[...], hi_lo(mine_ref[...] + got_ref[...])))
    out_ref[:, :cap, :] = rows.reshape(owners, cap, emb)
    out_ref[:, cap:, :] = srow_ref[...].reshape(owners, 8, emb)


def cold_kernel(cap, arrived_ref, table_ref, accum_ref, new_ref, acc_ref):
    slots, emb = table_ref.shape
    sub = iota((slots, cap), 0, F32)

    def body(d, acc):
        slot = arrived_ref[d, cap : cap + 1, :][:, :cap]
        hit = (sub == slot).astype(F32).astype(BF16)
        return acc + dot(hit, hi_lo(arrived_ref[d, :cap, :]))

    grad = sum_halves(loop(arrived_ref.shape[0], body, jnp.zeros((slots, 2 * emb), F32)))
    new_ref[...], acc_ref[...] = adagrad(table_ref[...], accum_ref[...], grad)


def final_kernel(mine_ref, theirs_ref, table_ref, accum_ref, new_ref, acc_ref):
    half = mine_ref.shape[0]
    core = lax.axis_index("mp") % 2
    for ref, c in ((mine_ref, core), (theirs_ref, 1 - core)):
        at = pl.ds(pl.multiple_of(c * half, half), half)
        new_ref[at, :], acc_ref[at, :] = adagrad(table_ref[at, :], accum_ref[at, :], ref[...])


def per_device(
    hot_ids,
    touched,
    cold_items,
    bag_counts,
    owner_map,
    grad_out,
    weight_in,
    bias_in,
    weight_out,
    hot_table,
    hot_accum,
    cold_table,
    cold_accum,
):
    dp_count = lax.axis_size("dp")
    mp_count = lax.axis_size("mp")
    slots, emb = cold_table.shape
    samples, fields = hot_ids.shape
    touch = touched.shape[2]
    items = cold_items.shape[2]
    d_in, hidden = weight_in.shape
    all_hidden = mp_count * hidden
    hot_rows = hot_table.shape[0]
    share = samples // mp_count
    cap = -(-(2 * touch // dp_count) // 8) * 8
    item_rows = items // emb
    count_rows = samples // emb
    both = ("dp", "mp")

    def swap(x, mask):
        return lax.ppermute(x, "mp", [(i, i ^ mask) for i in range(mp_count)])

    def far_swap(x, mask):
        return lax.ppermute(x, "dp", [(i, i ^ mask) for i in range(dp_count)])

    def near_swap(x, k):
        mask = k // 2 * mp_count + k % 2 * 2
        return lax.ppermute(x, both, [(i, i ^ mask) for i in range(dp_count * mp_count)])

    near = dp_count == 8 and mp_count == 4

    small = [
        owner_map.reshape(-1, emb),
        touched.reshape(1, touch),
        weight_out,
        cold_items.reshape(item_rows, emb),
        bag_counts.reshape(count_rows, emb),
        bias_in.reshape(1, hidden),
    ]
    own, *small = call(
        lambda *r: cast_kernel(1 + len(small), *r),
        [((slots, emb) if near else (dp_count, slots, emb), BF16, near)]
        + [(x.shape, x.dtype, True) for x in small],
        [cold_table, *small],
        raw=range(1 + len(small)),
        scratch=[
            pltpu.VMEM((slots, emb), F32),
            pltpu.SemaphoreType.DMA((1 + len(small),)),
        ],
    )
    map_rows, touched_row, *small = small
    if near:
        tables = [own]
        for k in (2, 4, 6):
            tables.append(far_swap(own, k))
    else:
        tables = lax.all_to_all(own, "dp", split_axis=0, concat_axis=0, tiled=True)

    w_far = swap(weight_in, 2)
    w_near = swap(weight_in, 1)
    weights = [weight_in, w_near, w_far, swap(w_far, 1)]
    at = pack_rows(weight_out.shape[1], hidden, emb, item_rows)
    (pack,) = call(lambda *r: prep_kernel(at, *r), [((at[-1], emb), BF16, True)], small)
    pack_far = swap(pack, 2)
    pack_near = swap(pack, 1)
    packs = [pack, pack_near, pack_far, swap(pack_far, 1)]

    pos, pos_row = call(
        lambda *r: place_kernel(mp_count, slots, *r),
        [((touch, emb), I32, True), ((8, touch), I32, True)],
        [map_rows, touched_row],
    )
    hot_near, ids_near, weight_near, grads_near = call(
        lambda *r: load_kernel(share, *r),
        [
            (hot_table.shape, F32, True),
            ((fields, samples), I32, True),
            (weight_in.shape, BF16, True),
            ((share, grad_out.shape[1]), BF16, True),
        ],
        [hot_table, hot_ids.T, weight_in, grad_out],
        raw=range(4),
        scratch=[pltpu.SemaphoreType.DMA((4,))],
    )
    weights[0] = weight_near

    def count(pair):
        return call(
            lambda *r: count_kernel(share, touch, at, item_rows, count_rows, *r),
            [((share, 2 * touch), BF16, True), ((2 * touch, share), BF16, True)],
            pair,
            scratch=[
                pltpu.VMEM((2, item_rows, emb), F32),
                pltpu.VMEM((2, count_rows, emb), F32),
                pltpu.VMEM((2, count_rows, emb), F32),
                pltpu.VMEM((touch, share), F32),
            ],
        )

    cnta, cntta = count(packs[:2])
    cntb, cnttb = count(packs[2:])

    oht, rows = call(
        lambda *r: onehot_kernel(share, fields, *r),
        [((hot_rows, fields * share), BF16, True), ((fields * emb, share), BF16, True)],
        [ids_near, hot_near],
    )

    wt, tail, pre, back = call(
        lambda *r: pre_kernel(share, at, hidden, *r),
        [
            ((all_hidden, d_in), BF16, True),
            ((emb, all_hidden), BF16, True),
            ((share, all_hidden), F32, True),
            ((share, all_hidden), F32, True),
        ],
        [*weights, *packs, grads_near, rows],
    )

    if near:
        other_row = far_swap(pos_row, 1)
        mine, give = call(
            fetch_near_kernel, [((touch, emb), BF16, True)] * 2, [pos, other_row, *tables]
        )
        from_near = near_swap(give, 2)
        from_far = near_swap(mine, 1)
        from_cross = near_swap(give, 3)
        (fetched,) = call(
            join_kernel, [((2, touch, emb), BF16, True)], [mine, from_near, from_far, from_cross]
        )
    else:
        (mine,) = call(fetch_kernel, [((touch, emb), BF16, True)], [pos, tables], late=(1,))
        fetched = jnp.stack([mine, swap(mine, 2)])
    fetched_core = swap(fetched, 1)

    half_rows = hot_rows // 2
    ig, bag, hot_send = call(
        lambda *r: main_kernel(fields, *r),
        [
            ((fields * share, 2 * emb), BF16, True),
            ((share, 2 * emb), BF16, True),
            ((half_rows, emb), F32, True),
        ],
        [cnta, cntb, fetched, fetched_core, pre, back, tail, wt, oht],
    )
    hot_got = swap(hot_send, 1)
    hot_keep, touch_send, touch_keep = call(
        keep_kernel,
        [
            ((half_rows, emb), F32, True),
            ((mp_count // 2, touch, emb), F32, True),
            ((mp_count // 2, touch, emb), F32, True),
        ],
        [oht, ig, bag, cntta, cnttb],
    )

    group_size = dp_count * mp_count // 2
    rank_groups = [[g * 2 + c for g in range(group_size)] for c in range(2)]

    def exchange(x):
        return lax.all_to_all(
            x, both, split_axis=0, concat_axis=0, tiled=True, axis_index_groups=rank_groups
        )

    if near:
        rows_each = half_rows // group_size
        shape = (group_size, rows_each, emb)
        line = (dp_count // 2, rows_each, emb)
        pieces = call(
            split_near_kernel,
            [(line, F32, True)] * 4,
            [hot_keep.reshape(shape), hot_got.reshape(shape)],
        )
        pieces = [near_swap(x, k) if k else x for k, x in enumerate(pieces)]
        (part,) = call(sum_kernel, [(line, F32, True)], pieces)
        pieces = [part]
        for k in (1, 2, 3):
            pieces.append(far_swap(part, 2 * k))
        (part,) = call(sum_kernel, [(line, F32, True)], pieces)
        pieces = [near_swap(part, k) if k else part for k in range(4)]
        (half,) = call(order_near_kernel, [(shape, F32, True)], pieces)
        half = half.reshape(half_rows, emb)
    else:
        (chip,) = call(add_kernel, [((half_rows, emb), F32, True)], [hot_keep, hot_got])
        parts = exchange(chip.reshape(group_size, -1, emb))
        (shard,) = call(reduce_kernel, [(parts.shape, F32, True)], [parts])
        half = exchange(shard).reshape(half_rows, emb)
    other = swap(half, 1)
    hot_updated, hot_accum_new = call(
        final_kernel, [(hot_table.shape, F32, False)] * 2, [half, other, hot_table, hot_accum]
    )

    q_mat, slot_rows = call(
        lambda *r: bucket_kernel(slots, cap, *r),
        [((dp_count * cap, touch), BF16, True), ((dp_count * 8, emb), F32, True)],
        [pos],
    )
    touch_got = swap(touch_send, 1)
    mine, give = call(pair_kernel, [((touch, emb), F32, True)] * 2, [touch_keep, touch_got])
    got = swap(give, 2)
    (outgoing,) = call(
        lambda *r: pack_kernel(cap, *r),
        [((dp_count, cap + 8, emb), F32, True)],
        [mine, got, q_mat, slot_rows],
    )
    arrived = lax.all_to_all(outgoing, "dp", split_axis=0, concat_axis=0, tiled=True)
    cold_updated, cold_accum_new = call(
        lambda *r: cold_kernel(cap, *r),
        [(cold_table.shape, F32, False)] * 2,
        [arrived, cold_table, cold_accum],
    )
    return (hot_updated, hot_accum_new, cold_updated, cold_accum_new)


def solution(mesh):
    return whole(mesh)


def whole(mesh):
    return jax.shard_map(
        per_device,
        mesh=mesh,
        in_specs=(
            P("dp", None),
            P("dp", "mp", None),
            P("dp", "mp", None),
            P("dp", "mp", None),
            P(),
            P("dp", None),
            P(None, "mp"),
            P("mp",),
            P("mp", None),
            P(),
            P(),
            P(("dp", "mp"), None),
            P(("dp", "mp"), None),
        ),
        out_specs=(P(), P(), P(("dp", "mp"), None), P(("dp", "mp"), None)),
        check_vma=False,
    )
```

```python
import jax
import jax.numpy as jnp
from jax import lax
from jax.experimental import pallas as pl
from jax.experimental.pallas import tpu as pltpu
from jax.sharding import PartitionSpec as P

STEP_SIZE = 0.5
F32 = jnp.float32
BF16 = jnp.bfloat16
I32 = jnp.int32


def adagrad(table_rows, accum_rows, grad_rows):
    accum_new = accum_rows + grad_rows * grad_rows
    return (table_rows - STEP_SIZE * grad_rows / jnp.sqrt(accum_new), accum_new)


def loop(count, body, init):
    if count <= 16:
        for i in range(count):
            init = body(i, init)
        return init
    return lax.fori_loop(0, count, body, init)


def hi_lo(x):
    hi = x.astype(BF16)
    lo = (x - hi.astype(F32)).astype(BF16)
    return jnp.concatenate([hi, lo], axis=1)


def sum_halves(x):
    half = x.shape[1] // 2
    return x[:, :half] + x[:, half:]


def dot(a, b, dims=(((1,), (0,)), ((), ()))):
    return lax.dot_general(a, b, dims, preferred_element_type=F32)


NT = (((1,), (1,)), ((), ()))
TN = (((0,), (0,)), ((), ()))


def iota(shape, dim, dtype=I32):
    r = lax.broadcasted_iota(I32, shape, dim)
    return r if dtype == I32 else r.astype(dtype)


VM = pl.BlockSpec(memory_space=pltpu.VMEM)
ANY = pl.BlockSpec(memory_space=pl.ANY)


def call(body, outs, ins, scratch=(), late=(), raw=(), sent=False):
    avals = [
        pltpu.VMEM(shape, dtype) if stay else jax.ShapeDtypeStruct(shape, dtype)
        for shape, dtype, stay in outs
    ]
    return pl.pallas_call(
        body,
        out_shape=avals,
        in_specs=[ANY if i in raw else VM for i in range(len(ins))],
        out_specs=[ANY if sent else VM] * len(outs),
        scratch_shapes=scratch,
        compiler_params=pltpu.CompilerParams(vmem_limit_bytes=16 * 1024 * 1024),
    )(
        *[
            pltpu.with_memory_space_constraint(
                x, pltpu.HBM if i in late or i in raw else pltpu.VMEM
            )
            for i, x in enumerate(ins)
        ]
    )


def column(row):
    return jnp.broadcast_to(row, (8, row.shape[1])).T[:, 0:1]


def cast_kernel(count, *refs):
    sources, outs = refs[:count], refs[count : 2 * count]
    table_ref, sems = refs[2 * count :]
    copies = [
        pltpu.make_async_copy(src, outs[i] if i else table_ref, sems.at[i])
        for i, src in enumerate(sources)
    ]
    for copy in copies:
        copy.start()
    copies[0].wait()
    table = table_ref[...].astype(BF16)
    if len(outs[0].shape) == 2:
        outs[0][...] = table
    else:
        for o in range(outs[0].shape[0]):
            outs[0][o] = table
    for copy in copies[1:]:
        copy.wait()


def pack_rows(out_width, hidden, emb, item_rows):
    starts = [0, out_width // emb * hidden]
    starts.append(starts[-1] + -(-item_rows // 16) * 16)
    starts.append(starts[-1] + 16)
    return starts + [starts[-1] + 16]


def prep_kernel(at, v_ref, items_ref, sizes_ref, bias_ref, out_ref):
    hidden, width = v_ref.shape
    emb = out_ref.shape[1]
    for j in range(width // emb):
        out_ref[j * hidden : (j + 1) * hidden, :] = v_ref[:, j * emb : (j + 1) * emb]

    def padded(x, rows):
        if x.shape[0] == rows:
            return x
        return jnp.concatenate([x, jnp.zeros((rows - x.shape[0], emb), F32)], axis=0)

    items = items_ref[...].astype(F32)
    out_ref[at[1] : at[2], :] = padded(items, at[2] - at[1]).astype(BF16)
    out_ref[at[2] : at[3], :] = padded(sizes_ref[...].astype(F32), 16).astype(BF16)
    bias = bias_ref[...]
    hi = bias.astype(BF16).astype(F32)
    mid = (bias - hi).astype(BF16).astype(F32)
    low = bias - hi - mid
    out_ref[at[3] : at[4], :] = padded(jnp.concatenate([hi, mid, low], axis=0), 16).astype(BF16)


def place_kernel(mp_count, slots, map_ref, ids_ref, pos_ref, row_ref):
    touch = ids_ref.shape[1]
    map_rows, lanes = map_ref.shape
    ids_col = column(ids_ref[...])
    in_row = (iota((touch, map_rows), 1) == ids_col // lanes).astype(F32)
    picked = lax.dot_general(
        in_row, map_ref[...].astype(F32), (((1,), (0,)), ((), ())),
        precision=lax.Precision.HIGHEST, preferred_element_type=F32,
    )
    in_lane = iota((touch, lanes), 1) == ids_col % lanes
    stored = jnp.sum(jnp.where(in_lane, picked, 0.0), axis=1, keepdims=True).astype(I32)
    stored = jnp.broadcast_to(stored, (touch, lanes))
    pos = stored // (mp_count * slots) * slots + stored % slots
    pos_ref[...] = pos
    row_ref[...] = pos.T[:8, :]


def load_kernel(
    share, hot_hbm, hot_ids_hbm, weight_hbm, grads_hbm,
    hot_ref, hot_ids_ref, weight_ref, grads_ref, sems,
):
    my = lax.axis_index("mp")
    mine = grads_hbm.at[pl.ds(pl.multiple_of(my * share, share), share), :]
    copies = [
        pltpu.make_async_copy(hot_hbm, hot_ref, sems.at[0]),
        pltpu.make_async_copy(hot_ids_hbm, hot_ids_ref, sems.at[1]),
        pltpu.make_async_copy(weight_hbm, weight_ref, sems.at[2]),
        pltpu.make_async_copy(mine, grads_ref, sems.at[3]),
    ]
    for copy in copies:
        copy.start()
    for copy in copies:
        copy.wait()


def count_kernel(
    share, touch, at, item_rows, count_rows, p0, p1, cnt_ref, cntt_ref,
    items_ref, starts_ref, ends_ref, acc_ref,
):
    lanes = p0.shape[1]
    my = lax.axis_index("mp")
    per = share // lanes
    block = min(item_rows, -(-3 * item_rows // 8))
    sub_t = iota((touch, lanes), 0, F32)
    upto = (iota((lanes, lanes), 0) <= iota((lanes, lanes), 1)).astype(F32).astype(BF16)
    packs = (p0, p1)
    for k, pack in enumerate(packs):
        sizes = pack[at[2] : at[3], :]
        ends = dot(sizes, upto)[:count_rows]
        sizes = sizes.astype(F32)[:count_rows]
        totals = jnp.broadcast_to(jnp.sum(sizes, axis=1, keepdims=True), ends.shape)
        row = iota(ends.shape, 0)
        for r in range(count_rows - 1):
            ends = ends + jnp.where(row > r, totals[r : r + 1, :], 0.0)
        ends_ref[k] = ends
        starts_ref[k] = ends - sizes
        items_ref[k] = pack[at[1] : at[2], :].astype(F32)[:item_rows]

    def rows_of(ref, k):
        return jnp.concatenate([ref[k, pl.ds(my * per + j, 1), :] for j in range(per)], axis=1)

    bounds = []
    for k in range(len(packs)):
        starts = rows_of(starts_ref, k)
        ends = rows_of(ends_ref, k)
        first = jnp.min(starts).astype(I32) // lanes
        last = (jnp.max(ends).astype(I32) + lanes - 1) // lanes
        bounds.append((starts, ends, jnp.minimum(first, item_rows - block), last))

    def counted(k, first, rows, starts, ends):
        pick = jnp.concatenate(
            [
                (sub_t == items_ref[k, pl.ds(first + j, 1), :]).astype(F32).astype(BF16)
                for j in range(rows)
            ],
            axis=1,
        )
        pos = iota((rows * lanes, share), 0, F32) + (first * lanes).astype(F32)
        memb = ((pos >= starts) & (pos < ends)).astype(F32).astype(BF16)
        return dot(pick, memb)

    for k, (starts, ends, first, last) in enumerate(bounds):
        acc_ref[...] = counted(k, first, block, starts, ends)

        def body(c, carry):
            acc_ref[...] += counted(k, c, 1, starts, ends)
            return carry

        lax.fori_loop(first + block, last, body, 0)
        counts_t = acc_ref[...]
        cntt_ref[k * touch : (k + 1) * touch, :] = counts_t.astype(BF16)
        cnt_ref[:, k * touch : (k + 1) * touch] = counts_t.T.astype(BF16)


def pre_kernel(
    share, at, hidden, w0, w1, w2, w3, p0, p1, p2, p3, grads_ref, rows_ref,
    wt_ref, tail_ref, pre_ref, back_ref,
):
    emb = p0.shape[1]
    hot_cols = rows_ref.shape[0]
    grads = grads_ref[...]
    rows = rows_ref[...]
    for k, (w, p) in enumerate(zip((w0, w1, w2, w3), (p0, p1, p2, p3))):
        cols = slice(k * hidden, (k + 1) * hidden)
        bias = jnp.sum(p[at[3] : at[4], :].astype(F32), axis=0, keepdims=True)
        pre_ref[:, cols] = dot(rows, w[:hot_cols, :], TN) + bias
        back = jnp.zeros((share, hidden), F32)
        for j in range(grads.shape[1] // emb):
            piece = p[j * hidden : (j + 1) * hidden, :]
            back = back + dot(grads[:, j * emb : (j + 1) * emb], piece, NT)
        back_ref[:, cols] = back
        tail_ref[:, cols] = w[hot_cols:, :]
        wt_ref[cols, :] = w[...].astype(F32).T.astype(BF16)


def fetch_kernel(pos_ref, table_ref, out_ref):
    owners, slots, _ = table_ref.shape

    def body(o, acc):
        return acc + dot(hits(pos_ref[...], o * slots, slots), table_ref[o])

    out_ref[...] = loop(owners, body, jnp.zeros(out_ref.shape, F32)).astype(BF16)


def fetch_near_kernel(pos_ref, row_ref, *refs):
    tables, (mine_ref, give_ref) = refs[:-2], refs[-2:]
    touch, lanes = pos_ref.shape
    slots = tables[0].shape[0]
    my = lax.axis_index("dp")
    theirs = jnp.broadcast_to(row_ref[...].T[:, 0:1], (touch, lanes))
    both = jnp.concatenate([pos_ref[...], theirs], axis=0)
    acc = jnp.zeros((2 * touch, mine_ref.shape[1]), F32)
    for k, table in enumerate(tables):
        acc = acc + dot(hits(both, (my ^ (2 * k)) * slots, slots), table[...])
    mine_ref[...] = acc[:touch].astype(BF16)
    give_ref[...] = acc[touch:].astype(BF16)


def join_kernel(mine_ref, near_ref, far_ref, cross_ref, out_ref):
    out_ref[0] = (mine_ref[...].astype(F32) + near_ref[...].astype(F32)).astype(BF16)
    out_ref[1] = (far_ref[...].astype(F32) + cross_ref[...].astype(F32)).astype(BF16)


def hits(pos, first, slots):
    rel = pos - first
    lane = iota(rel.shape, 1)
    lanes = rel.shape[1]
    return jnp.concatenate(
        [(lane + j * lanes == rel).astype(F32).astype(BF16) for j in range(slots // lanes)], axis=1
    )


def onehot_kernel(share, fields, ids_ref, hot_ref, out_ref, rows_ref):
    my = lax.axis_index("mp")
    emb = hot_ref.shape[1]
    hot = hot_ref[...].T.astype(BF16)
    sub = iota((out_ref.shape[0], share), 0)
    for f in range(fields):
        mine = ids_ref[f : f + 1, pl.ds(pl.multiple_of(my * share, share), share)]
        hit = (sub == mine).astype(F32).astype(BF16)
        out_ref[:, f * share : (f + 1) * share] = hit
        rows_ref[f * emb : (f + 1) * emb, :] = dot(hot, hit).astype(BF16)


def bucket_kernel(slots, cap, pos_ref, q_ref, srow_ref):
    pos = pos_ref[...]
    touch, lanes = pos.shape
    row = pos.T[0:1, :]
    owner = row // slots
    before = iota((touch, touch), 0) < iota((touch, touch), 1)
    rank = jnp.sum(
        ((pos[:, 0:1] // slots == owner) & before).astype(F32), axis=0, keepdims=True
    )
    bucket = owner.astype(F32) * float(cap) + rank
    q_ref[...] = (iota(q_ref.shape, 0, F32) == bucket).astype(F32).astype(BF16)
    at_rank = (iota((touch, lanes), 1, F32) == column(rank)).astype(F32)
    mine = jnp.where(
        iota((srow_ref.shape[0], touch), 0) // 8 == owner, (row % slots).astype(F32), 0.0
    )
    srow_ref[...] = lax.dot_general(
        mine, at_rank, (((1,), (0,)), ((), ())),
        precision=lax.Precision.HIGHEST, preferred_element_type=F32,
    )


def main_kernel(
    fields, cnta_ref, cntb_ref, mine_ref, core_ref, pre_ref, back_ref, tail_ref, wt_ref, oht_ref,
    ig_ref, bag_ref, send_ref,
):
    _, touch, emb = mine_ref.shape
    share = cnta_ref.shape[0]
    core = lax.axis_index("mp") % 2
    pooled = jnp.zeros((share, emb), F32)
    for k in range(4):
        cnt = (cnta_ref, cntb_ref)[k // 2]
        rows = (mine_ref, core_ref)[k % 2][k // 2]
        pooled = pooled + dot(cnt[:, k % 2 * touch : (k % 2 + 1) * touch], rows)
    pre = pre_ref[...] + dot(pooled.astype(BF16), tail_ref[...])
    sig = jax.nn.sigmoid(pre)
    hidden = (back_ref[...] * sig * (1.0 + pre * (1.0 - sig))).astype(BF16)
    grad = dot(hidden, wt_ref[...])
    for f in range(fields):
        ig_ref[f * share : (f + 1) * share, :] = hi_lo(grad[:, f * emb : (f + 1) * emb])
    bag_ref[...] = hi_lo(grad[:, fields * emb :])
    half = send_ref.shape[0]
    first = pl.multiple_of((1 - core) * half, half)
    send_ref[...] = sum_halves(dot(oht_ref[pl.ds(first, half), :], ig_ref[...]))


def keep_kernel(oht_ref, ig_ref, bag_ref, cntta_ref, cnttb_ref, keep_ref, touch_send, touch_keep):
    half = keep_ref.shape[0]
    core = lax.axis_index("mp") % 2
    first = pl.multiple_of(core * half, half)
    keep_ref[...] = sum_halves(dot(oht_ref[pl.ds(first, half), :], ig_ref[...]))
    touch = touch_send.shape[1]
    for k in range(4):
        ref = touch_send if k % 2 else touch_keep
        counts = (cntta_ref, cnttb_ref)[k // 2]
        rows = slice(k % 2 * touch, (k % 2 + 1) * touch)
        ref[k // 2] = sum_halves(dot(counts[rows, :], bag_ref[...]))


def add_kernel(a_ref, b_ref, out_ref):
    out_ref[...] = a_ref[...] + b_ref[...]


def pair_kernel(keep_ref, got_ref, mine_ref, give_ref):
    mine_ref[...] = keep_ref[0] + got_ref[0]
    give_ref[...] = keep_ref[1] + got_ref[1]


def fetch_kernel(pos_ref, table_ref, out_ref):
    owners, slots, emb = table_ref.shape
    touch, lanes = pos_ref.shape
    lane = iota((touch, lanes), 1)

    def body(o, acc):
        rel = pos_ref[...] - o * slots
        hit = jnp.concatenate(
            [
                (lane + j * lanes == rel).astype(F32).astype(BF16)
                for j in range(slots // lanes)
            ],
            axis=1,
        )
        return acc + dot(hit, table_ref[o])

    out_ref[...] = loop(owners, body, jnp.zeros((touch, emb), F32)).astype(BF16)


def reduce_kernel(parts_ref, out_ref):
    total = jnp.sum(parts_ref[...], axis=0, keepdims=True)
    out_ref[...] = jnp.broadcast_to(total, out_ref.shape)


def near_place(far, k):
    near = lax.axis_index("dp") % 2
    group = lax.axis_index("mp") // 2
    return (far * 2 + (near ^ (k // 2))) * 2 + (group ^ (k % 2))


def split_near_kernel(keep_ref, got_ref, *outs):
    for k, ref in enumerate(outs):
        for far in range(ref.shape[0]):
            at = near_place(far, k)
            ref[far] = keep_ref[at] + got_ref[at]


def sum_kernel(a_ref, b_ref, c_ref, d_ref, out_ref):
    out_ref[...] = (a_ref[...] + b_ref[...]) + (c_ref[...] + d_ref[...])


def order_near_kernel(*refs):
    for k, ref in enumerate(refs[:-1]):
        for far in range(ref.shape[0]):
            refs[-1][near_place(far, k)] = ref[far]


def pack_kernel(cap, mine_ref, got_ref, q_ref, srow_ref, out_ref):
    owners = out_ref.shape[0]
    emb = out_ref.shape[2]
    rows = sum_halves(dot(q_ref[...], hi_lo(mine_ref[...] + got_ref[...])))
    out_ref[:, :cap, :] = rows.reshape(owners, cap, emb)
    out_ref[:, cap:, :] = srow_ref[...].reshape(owners, 8, emb)


def cold_kernel(cap, arrived_ref, table_ref, accum_ref, new_ref, acc_ref):
    slots, emb = table_ref.shape
    sub = iota((slots, cap), 0, F32)

    def body(d, acc):
        slot = arrived_ref[d, cap : cap + 1, :][:, :cap]
        hit = (sub == slot).astype(F32).astype(BF16)
        return acc + dot(hit, hi_lo(arrived_ref[d, :cap, :]))

    grad = sum_halves(loop(arrived_ref.shape[0], body, jnp.zeros((slots, 2 * emb), F32)))
    new_ref[...], acc_ref[...] = adagrad(table_ref[...], accum_ref[...], grad)


def final_kernel(mine_ref, theirs_ref, table_ref, accum_ref, new_hbm, acc_hbm, new_ref, acc_ref, sems):
    half = mine_ref.shape[0]
    parts = sems.shape[1] // 2
    rows = half // parts
    core = lax.axis_index("mp") % 2
    copies = []
    for i, (ref, c) in enumerate(((mine_ref, core), (theirs_ref, 1 - core))):
        for j in range(parts):
            at = pl.ds(pl.multiple_of(c * half + j * rows, rows), rows)
            new_ref[at, :], acc_ref[at, :] = adagrad(
                table_ref[at, :], accum_ref[at, :], ref[j * rows : (j + 1) * rows, :]
            )
            k = i * parts + j
            copies.append(pltpu.make_async_copy(new_ref.at[at, :], new_hbm.at[at, :], sems.at[0, k]))
            copies.append(pltpu.make_async_copy(acc_ref.at[at, :], acc_hbm.at[at, :], sems.at[1, k]))
            copies[-2].start()
            copies[-1].start()
    for copy in copies:
        copy.wait()


def per_device(
    hot_ids,
    touched,
    cold_items,
    bag_counts,
    owner_map,
    grad_out,
    weight_in,
    bias_in,
    weight_out,
    hot_table,
    hot_accum,
    cold_table,
    cold_accum,
):
    dp_count = lax.axis_size("dp")
    mp_count = lax.axis_size("mp")
    slots, emb = cold_table.shape
    samples, fields = hot_ids.shape
    touch = touched.shape[2]
    items = cold_items.shape[2]
    d_in, hidden = weight_in.shape
    all_hidden = mp_count * hidden
    hot_rows = hot_table.shape[0]
    share = samples // mp_count
    cap = -(-(2 * touch // dp_count) // 8) * 8
    item_rows = items // emb
    count_rows = samples // emb
    both = ("dp", "mp")

    def swap(x, mask):
        return lax.ppermute(x, "mp", [(i, i ^ mask) for i in range(mp_count)])

    def far_swap(x, mask):
        return lax.ppermute(x, "dp", [(i, i ^ mask) for i in range(dp_count)])

    def near_swap(x, k):
        mask = k // 2 * mp_count + k % 2 * 2
        return lax.ppermute(x, both, [(i, i ^ mask) for i in range(dp_count * mp_count)])

    near = dp_count == 8 and mp_count == 4

    small = [
        owner_map.reshape(-1, emb),
        touched.reshape(1, touch),
        weight_out,
        cold_items.reshape(item_rows, emb),
        bag_counts.reshape(count_rows, emb),
        bias_in.reshape(1, hidden),
    ]
    own, *small = call(
        lambda *r: cast_kernel(1 + len(small), *r),
        [((slots, emb) if near else (dp_count, slots, emb), BF16, near)]
        + [(x.shape, x.dtype, True) for x in small],
        [cold_table, *small],
        raw=range(1 + len(small)),
        scratch=[
            pltpu.VMEM((slots, emb), F32),
            pltpu.SemaphoreType.DMA((1 + len(small),)),
        ],
    )
    map_rows, touched_row, *small = small
    if near:
        tables = [own]
        for k in (2, 4, 6):
            tables.append(far_swap(own, k))
    else:
        tables = lax.all_to_all(own, "dp", split_axis=0, concat_axis=0, tiled=True)

    w_far = swap(weight_in, 2)
    w_near = swap(weight_in, 1)
    weights = [weight_in, w_near, w_far, swap(w_far, 1)]
    at = pack_rows(weight_out.shape[1], hidden, emb, item_rows)
    (pack,) = call(lambda *r: prep_kernel(at, *r), [((at[-1], emb), BF16, True)], small)
    pack_far = swap(pack, 2)
    pack_near = swap(pack, 1)
    packs = [pack, pack_near, pack_far, swap(pack_far, 1)]

    pos, pos_row = call(
        lambda *r: place_kernel(mp_count, slots, *r),
        [((touch, emb), I32, True), ((8, touch), I32, True)],
        [map_rows, touched_row],
    )
    hot_near, ids_near, weight_near, grads_near = call(
        lambda *r: load_kernel(share, *r),
        [
            (hot_table.shape, F32, True),
            ((fields, samples), I32, True),
            (weight_in.shape, BF16, True),
            ((share, grad_out.shape[1]), BF16, True),
        ],
        [hot_table, hot_ids.T, weight_in, grad_out],
        raw=range(4),
        scratch=[pltpu.SemaphoreType.DMA((4,))],
    )
    weights[0] = weight_near

    def count(pair):
        return call(
            lambda *r: count_kernel(share, touch, at, item_rows, count_rows, *r),
            [((share, 2 * touch), BF16, True), ((2 * touch, share), BF16, True)],
            pair,
            scratch=[
                pltpu.VMEM((2, item_rows, emb), F32),
                pltpu.VMEM((2, count_rows, emb), F32),
                pltpu.VMEM((2, count_rows, emb), F32),
                pltpu.VMEM((touch, share), F32),
            ],
        )

    cnta, cntta = count(packs[:2])
    cntb, cnttb = count(packs[2:])

    oht, rows = call(
        lambda *r: onehot_kernel(share, fields, *r),
        [((hot_rows, fields * share), BF16, True), ((fields * emb, share), BF16, True)],
        [ids_near, hot_near],
    )

    wt, tail, pre, back = call(
        lambda *r: pre_kernel(share, at, hidden, *r),
        [
            ((all_hidden, d_in), BF16, True),
            ((emb, all_hidden), BF16, True),
            ((share, all_hidden), F32, True),
            ((share, all_hidden), F32, True),
        ],
        [*weights, *packs, grads_near, rows],
    )

    if near:
        other_row = far_swap(pos_row, 1)
        mine, give = call(
            fetch_near_kernel, [((touch, emb), BF16, True)] * 2, [pos, other_row, *tables]
        )
        from_near = near_swap(give, 2)
        from_far = near_swap(mine, 1)
        from_cross = near_swap(give, 3)
        (fetched,) = call(
            join_kernel, [((2, touch, emb), BF16, True)], [mine, from_near, from_far, from_cross]
        )
    else:
        (mine,) = call(fetch_kernel, [((touch, emb), BF16, True)], [pos, tables], late=(1,))
        fetched = jnp.stack([mine, swap(mine, 2)])
    fetched_core = swap(fetched, 1)

    half_rows = hot_rows // 2
    ig, bag, hot_send = call(
        lambda *r: main_kernel(fields, *r),
        [
            ((fields * share, 2 * emb), BF16, True),
            ((share, 2 * emb), BF16, True),
            ((half_rows, emb), F32, True),
        ],
        [cnta, cntb, fetched, fetched_core, pre, back, tail, wt, oht],
    )
    hot_got = swap(hot_send, 1)
    hot_keep, touch_send, touch_keep = call(
        keep_kernel,
        [
            ((half_rows, emb), F32, True),
            ((mp_count // 2, touch, emb), F32, True),
            ((mp_count // 2, touch, emb), F32, True),
        ],
        [oht, ig, bag, cntta, cnttb],
    )

    group_size = dp_count * mp_count // 2
    rank_groups = [[g * 2 + c for g in range(group_size)] for c in range(2)]

    def exchange(x):
        return lax.all_to_all(
            x, both, split_axis=0, concat_axis=0, tiled=True, axis_index_groups=rank_groups
        )

    if near:
        rows_each = half_rows // group_size
        shape = (group_size, rows_each, emb)
        line = (dp_count // 2, rows_each, emb)
        pieces = call(
            split_near_kernel,
            [(line, F32, True)] * 4,
            [hot_keep.reshape(shape), hot_got.reshape(shape)],
        )
        pieces = [near_swap(x, k) if k else x for k, x in enumerate(pieces)]
        (part,) = call(sum_kernel, [(line, F32, True)], pieces)
        pieces = [part]
        for k in (1, 2, 3):
            pieces.append(far_swap(part, 2 * k))
        (part,) = call(sum_kernel, [(line, F32, True)], pieces)
        pieces = [near_swap(part, k) if k else part for k in range(4)]
        (half,) = call(order_near_kernel, [(shape, F32, True)], pieces)
        half = half.reshape(half_rows, emb)
    else:
        (chip,) = call(add_kernel, [((half_rows, emb), F32, True)], [hot_keep, hot_got])
        parts = exchange(chip.reshape(group_size, -1, emb))
        (shard,) = call(reduce_kernel, [(parts.shape, F32, True)], [parts])
        half = exchange(shard).reshape(half_rows, emb)
    other = swap(half, 1)
    hot_updated, hot_accum_new = call(
        final_kernel,
        [(hot_table.shape, F32, False)] * 2,
        [half, other, hot_table, hot_accum],
        scratch=[
            pltpu.VMEM(hot_table.shape, F32),
            pltpu.VMEM(hot_table.shape, F32),
            pltpu.SemaphoreType.DMA((2, 4)),
        ],
        sent=True,
    )

    q_mat, slot_rows = call(
        lambda *r: bucket_kernel(slots, cap, *r),
        [((dp_count * cap, touch), BF16, True), ((dp_count * 8, emb), F32, True)],
        [pos],
    )
    touch_got = swap(touch_send, 1)
    mine, give = call(pair_kernel, [((touch, emb), F32, True)] * 2, [touch_keep, touch_got])
    got = swap(give, 2)
    (outgoing,) = call(
        lambda *r: pack_kernel(cap, *r),
        [((dp_count, cap + 8, emb), F32, True)],
        [mine, got, q_mat, slot_rows],
    )
    arrived = lax.all_to_all(outgoing, "dp", split_axis=0, concat_axis=0, tiled=True)
    cold_updated, cold_accum_new = call(
        lambda *r: cold_kernel(cap, *r),
        [(cold_table.shape, F32, False)] * 2,
        [arrived, cold_table, cold_accum],
    )
    return (hot_updated, hot_accum_new, cold_updated, cold_accum_new)


def solution(mesh):
    return whole(mesh)


def whole(mesh):
    return jax.shard_map(
        per_device,
        mesh=mesh,
        in_specs=(
            P("dp", None),
            P("dp", "mp", None),
            P("dp", "mp", None),
            P("dp", "mp", None),
            P(),
            P("dp", None),
            P(None, "mp"),
            P("mp",),
            P("mp", None),
            P(),
            P(),
            P(("dp", "mp"), None),
            P(("dp", "mp"), None),
        ),
        out_specs=(P(), P(), P(("dp", "mp"), None), P(("dp", "mp"), None)),
        check_vma=False,
    )
```
